32 devices in a mesh: groups: 2 (over x), space: 16 (over z, y, core).
Axes of the slice: x: 2, y: 2, z: 4, core: 2. Of those that a mesh axis runs over, the one named last changes fastest.
Arguments:
- volume: bfloat16 [96, 8, 8, 16, 128], P(('groups', 'space')), parts along dimension 0, may hold values from -6 to 6
- labels: int32 [96, 1024], P(('groups', 'space')), parts along dimension 0, may hold values 0 or 1
- run_lengths: int32 [4, 4], P('groups'), parts along dimension 0, may hold values from 1 to 3, 10 in all within a row
- run_owner: int32 [32], P('groups'), parts along dimension 0, may hold values from 0 to 15, each once
- reduce_one: bfloat16 [32, 128], replicated, may hold values from -0.5 to 0.5
- core_one: bfloat16 [27, 1024], replicated, may hold values from -0.21875 to 0.21875
- expand_one: bfloat16 [32, 128], replicated, may hold values from -1 to 1
- reduce_two: bfloat16 [32, 128], replicated, may hold values from -0.5 to 0.5
- core_two: bfloat16 [27, 1024], replicated, may hold values from -0.21875 to 0.21875
- expand_two: bfloat16 [32, 128], replicated, may hold values from -1 to 1
- head_vector: bfloat16 [128], replicated, may hold values from -0.5 to 0.5
Outputs:
- fault_prob: float32 [96, 1024], P(('groups', 'space')), parts along dimension 0
- reduce_one_grad: float32 [64, 128], P('groups'), parts along dimension 0
- core_one_grad: float32 [54, 1024], P('groups'), parts along dimension 0
- expand_one_grad: float32 [64, 128], P('groups'), parts along dimension 0
- reduce_two_grad: float32 [64, 128], P('groups'), parts along dimension 0
- core_two_grad: float32 [54, 1024], P('groups'), parts along dimension 0
- expand_two_grad: float32 [64, 128], P('groups'), parts along dimension 0
- head_grad: float32 [256], P('groups'), parts along dimension 0
The draws below stay inside these ranges and needn't reach their ends.
There are 2 independent parts, one for each index of `groups`. The reference program is written for one: setup_inputs(seed, part) draws one part's arguments, and reference() takes and returns one part's arrays. A program takes and returns all parts, laid end to end along the dimension named above; an argument that names none is the same for every part. Nothing has to cross between parts.
Inputs may be any that keep to these rules, and one draw needn't show every extreme that they name: run_lengths[j] cuts both crossline rows 2j and 2j+1, each of 10 pillars, into 4 runs in order from the low inline end; every row has a run of exactly 3 pillars. A permutation: run k (crossline row k // 4, the (k % 4)-th run of that row) is held by device run_owner[k] of the space axis, its pillars in that device's slots 0, 1, ... in inline order.
All inputs are finite; a program needn't handle non-finite values. No bound on the sum of `labels` on one device may be relied on, other than what follows from the above.
Results may differ from the reference program's by a relative error of at most 0.0049.
Values may be sent and summed in bfloat16 or wider, within the bound.
No kernel may reach another device: no remote copies, remote signals or barrier semaphores. Data moves between devices by JAX's collectives and lax.ppermute only.
A program may use at most 128 MiB of HBM per device.

```python
import math
import jax
import jax.numpy as jnp
import numpy as np
from jax import lax

C = 128
R = 32
E = 8
R_ROW = 4
PMAX = 3
TE = 16
PCELLS = 1024
ROWS = 4
PAIRS = 2
ROW_PILLARS = 10
N_SPACE = 16


def set_ends(array, key, smallest, largest):
    shape = array.shape
    place = [jax.random.randint(jax.random.fold_in(key, axis), (), 0, shape[axis]) for axis in range(len(shape))]
    array = array.at[tuple(place)].set(smallest)
    longest = shape.index(max(shape))
    place[longest] = (place[longest] + 1) % shape[longest]
    return array.at[tuple(place)].set(largest)


def block_scale(key, dims, split, smallest, high):
    factor_of, own = 1.0, jax.random.fold_in(key, 6)
    for axis_at, blocks in split:
        heights = jnp.exp(jax.random.uniform(jax.random.fold_in(own, axis_at), (blocks,), jnp.float32, smallest / len(split), high / len(split)))
        factor_of = factor_of * jnp.repeat(heights, dims[axis_at] // blocks).reshape([-1 if axis == axis_at else 1 for axis in range(len(dims))])
    return factor_of


def split_up(number_of, total, most, slope):
    weights = [(1 << 20) // math.isqrt(standing ** slope) + 1 for standing in range(2, number_of + 1)]
    surplus, holding = total - most - (number_of - 1), [1] * (number_of - 1)
    while surplus > 0:
        movable = [i for i in range(number_of - 1) if holding[i] < most]
        pool, budget = sum([weights[i] for i in movable]), surplus
        for i in movable:
            addition = min(most - holding[i], max(1, budget * weights[i] // pool), surplus)
            holding[i] = holding[i] + addition
            surplus = surplus - addition
    return np.array([most] + holding)


def uneven_parts(rng, amount, total, limit, skew):
    if amount == 2:
        one = jax.random.randint(rng, (), max(1, total - limit), min(limit, total - 1) + 1)
        return jnp.stack([one, total - one])
    sizes = jnp.asarray(split_up(amount, total, limit, skew), jnp.int32)
    pairs = (amount - 1) // 2
    source_of, sink = sizes[1:1 + 2 * pairs:2], sizes[2:2 + 2 * pairs:2]
    room = jnp.minimum(source_of - 1, limit - sink)
    moved = jax.random.randint(jax.random.fold_in(rng, 1), (pairs,), 0, 1 << 20) % (room + 1)
    sizes = sizes.at[1:1 + 2 * pairs:2].set(source_of - moved).at[2:2 + 2 * pairs:2].set(sink + moved)
    return sizes[jax.random.permutation(jax.random.fold_in(rng, 2), amount)]


def centred(rng, shape, scale, most, split=(), held_as=jnp.bfloat16):
    level = block_scale(rng, shape, split, -0.22, 0.18) if split else 1.0
    drawn = jax.random.normal(rng, shape, jnp.float32) * scale * level
    return jnp.minimum(jnp.maximum(drawn, -most), most).astype(held_as)


def setup_inputs(seed: int = 0, part: int = 0) -> dict:
    key_list = jax.random.split(jax.random.key(seed), 12)
    own_keys = jax.random.split(jax.random.fold_in(key_list[11], part), 12)
    return {
        "volume": centred(own_keys[0], (N_SPACE * PMAX, E, E, TE, C), 1.0, 6.0, ((0, 16),)),
        "labels": set_ends((jax.random.randint(own_keys[1], (N_SPACE * PMAX, PCELLS), 0, 3) < 1).astype(jnp.int32), jax.random.fold_in(own_keys[1], 1), 0, 1),
        "run_lengths": jax.vmap(lambda own: uneven_parts(own, R_ROW, ROW_PILLARS, PMAX, 2))(jax.random.split(own_keys[2], PAIRS)).reshape((PAIRS, R_ROW)).astype(jnp.int32),
        "run_owner": jax.random.permutation(own_keys[3], N_SPACE).astype(jnp.int32),
        "reduce_one": centred(key_list[4], (R, C), C ** -0.5, 0.5),
        "core_one": centred(key_list[5], (27, R * R), (27 * R) ** -0.5, 0.21875),
        "expand_one": centred(key_list[6], (R, C), R ** -0.5, 1.0),
        "reduce_two": centred(key_list[7], (R, C), C ** -0.5, 0.5),
        "core_two": centred(key_list[8], (27, R * R), (27 * R) ** -0.5, 0.21875),
        "expand_two": centred(key_list[9], (R, C), R ** -0.5, 1.0),
        "head_vector": centred(key_list[10], (C,), C ** -0.5, 0.5),
    }


OFFSETS = tuple((along_inline, along_cross, along_time) for along_inline in (-1, 0, 1) for along_cross in (-1, 0, 1) for along_time in (-1, 0, 1))


def pillar_table(run_lengths, run_owner):
    row_lengths = jnp.repeat(run_lengths, 2, axis=0).astype(jnp.int32)
    run_starts = (jnp.cumsum(row_lengths, axis=1) - row_lengths).astype(jnp.int32)
    places = jnp.arange(ROW_PILLARS, dtype=jnp.int32)
    run_index = (jnp.sum((run_starts[:, None, :] <= places[None, :, None]).astype(jnp.int32), axis=2) - 1).astype(jnp.int32)
    run_first = jnp.take_along_axis(run_starts, run_index, axis=1).astype(jnp.int32)
    global_run = (jnp.arange(ROWS, dtype=jnp.int32)[:, None] * R_ROW + run_index).astype(jnp.int32)
    return (run_owner[global_run] * PMAX + places[None, :] - run_first).astype(jnp.int32)


def slots_to_grid(per_slot, table):
    picked = per_slot[table.reshape(-1)]
    picked = picked.reshape((ROWS, ROW_PILLARS) + per_slot.shape[1:])
    axes_order = (1, 2, 0) + tuple(range(3, picked.ndim))
    moved = jnp.transpose(picked, axes_order)
    return moved.reshape((ROW_PILLARS * E, ROWS * E) + per_slot.shape[3:])


def grid_to_slots(gridded, table):
    pieces = gridded.reshape(ROW_PILLARS, E, ROWS, E, TE)
    pieces = jnp.transpose(pieces, (2, 0, 1, 3, 4)).reshape(ROWS * ROW_PILLARS, PCELLS)
    return jnp.zeros((N_SPACE * PMAX, PCELLS), jnp.float32).at[table.reshape(-1)].set(pieces)


def round_half(values):
    return lax.optimization_barrier(values.astype(jnp.bfloat16)).astype(jnp.float32)


def window_at(padded, offset, direction):
    lower_inline = 1 + direction * offset[0]
    lower_cross = 1 + direction * offset[1]
    lower_time = 1 + direction * offset[2]
    return padded[lower_inline:lower_inline + padded.shape[0] - 2, lower_cross:lower_cross + padded.shape[1] - 2, lower_time:lower_time + padded.shape[2] - 2, :]


def convolve(source, kernel, direction, transposed):
    padded = jnp.pad(source, ((1, 1), (1, 1), (1, 1), (0, 0)))
    result = jnp.zeros(source.shape, jnp.float32)
    for number, offset in enumerate(OFFSETS):
        matrix = kernel[number].reshape(R, R)
        window = window_at(padded, offset, direction)
        if transposed:
            result = result + jnp.einsum("abcs,rs->abcr", window, matrix)
        else:
            result = result + jnp.einsum("abcr,rs->abcs", window, matrix)
    return result


def core_gradient(source, upstream):
    padded = jnp.pad(source, ((1, 1), (1, 1), (1, 1), (0, 0)))
    pieces = [jnp.einsum("abcr,abcs->rs", window_at(padded, offset, 1), upstream).reshape(R * R) for offset in OFFSETS]
    return jnp.stack(pieces)


def silu_slope(values):
    sigmoid = jax.nn.sigmoid(values)
    return sigmoid * (1.0 + values * (1.0 - sigmoid))


def layer_forward(source, reduce_weight, core_weight, expand_weight):
    reduced = round_half(jnp.einsum("abcx,rx->abcr", source, reduce_weight))
    mixed = round_half(convolve(reduced, core_weight, 1, False))
    expanded = jnp.einsum("abcr,rx->abcx", mixed, expand_weight)
    output = round_half(source + jax.nn.silu(expanded))
    return reduced, mixed, expanded, output


def layer_backward(upstream, source, reduced, mixed, expanded, reduce_weight, core_weight, expand_weight):
    delta = round_half(upstream * silu_slope(expanded))
    expand_grad = jnp.einsum("abcr,abcx->rx", mixed, delta)
    mixed_grad = round_half(jnp.einsum("abcx,rx->abcr", delta, expand_weight))
    core_grad = core_gradient(reduced, mixed_grad)
    reduced_grad = round_half(convolve(mixed_grad, core_weight, -1, True))
    reduce_grad = jnp.einsum("abcr,abcx->rx", reduced_grad, source)
    passed = jnp.einsum("abcr,rx->abcx", reduced_grad, reduce_weight)
    return reduce_grad, core_grad, expand_grad, passed


def reference(volume, labels, run_lengths, run_owner, reduce_one, core_one, expand_one, reduce_two, core_two, expand_two, head_vector):
    table = pillar_table(run_lengths, run_owner)
    inputs = slots_to_grid(volume, table).astype(jnp.float32)
    targets = slots_to_grid(labels.reshape(N_SPACE * PMAX, E, E, TE), table).astype(jnp.float32)
    reduce_a = reduce_one.astype(jnp.float32)
    core_a = core_one.astype(jnp.float32)
    expand_a = expand_one.astype(jnp.float32)
    reduce_b = reduce_two.astype(jnp.float32)
    core_b = core_two.astype(jnp.float32)
    expand_b = expand_two.astype(jnp.float32)
    head_f = head_vector.astype(jnp.float32)
    reduced_a, mixed_a, expanded_a, hidden_a = layer_forward(inputs, reduce_a, core_a, expand_a)
    reduced_b, mixed_b, expanded_b, hidden_b = layer_forward(hidden_a, reduce_b, core_b, expand_b)
    logits = jnp.einsum("abcx,x->abc", hidden_b, head_f)
    chance = jax.nn.sigmoid(logits)
    differ = chance - targets
    head_grad = jnp.einsum("abcx,abc->x", hidden_b, differ)
    upstream_b = differ[..., None] * head_f
    grads_b = layer_backward(upstream_b, hidden_a, reduced_b, mixed_b, expanded_b, reduce_b, core_b, expand_b)
    upstream_a = upstream_b + grads_b[3]
    grads_a = layer_backward(upstream_a, inputs, reduced_a, mixed_a, expanded_a, reduce_a, core_a, expand_a)
    fault_prob = grid_to_slots(chance, table)
    return (fault_prob, grads_a[0] / PCELLS, grads_a[1] / PCELLS, grads_a[2] / PCELLS, grads_b[0] / PCELLS, grads_b[1] / PCELLS, grads_b[2] / PCELLS, head_grad / PCELLS)
```

```python
import functools

import jax
import jax.numpy as jnp
from jax import lax
from jax.experimental import pallas as pl
from jax.experimental.pallas import tpu as pltpu
from jax.sharding import PartitionSpec as P

BF = jnp.bfloat16
F32 = jnp.float32
SUB = 8
LIMIT = 40 * 1024 * 1024


class Dims:
    def __init__(self, nspace, slots, edge, times, channels, rank, pairs, row_runs):
        self.nspace, self.slots, self.edge, self.times = nspace, slots, edge, times
        self.channels, self.rank, self.pairs, self.row_runs = channels, rank, pairs, row_runs
        self.lanes = channels
        self.group = channels // rank
        self.tiles = times // self.group
        self.width = slots * edge
        self.rows = edge * self.width
        self.line = self.width + SUB
        self.lines = edge + 2
        self.span = self.lines * self.line
        self.core_rows = edge * self.line
        self.cells = edge * edge * times
        self.taps = 9
        self.t_send = 5
        self.t_recv = self.t_send + 2 * (1 + row_runs)
        self.t_size = self.t_recv + 2 * 3 * (slots + 2)
        self.block = (slots, self.tiles * SUB, channels)
        per_row = rank * rank // channels
        sizes = [27 * per_row, 27 * per_row, rank, rank, rank, rank, SUB]
        self.offsets = [sum(sizes[:i]) for i in range(len(sizes) + 1)]
        self.share = -(-self.offsets[-1] // (nspace * SUB)) * SUB


def dot(a, b):
    return lax.dot_general(a, b, (((1,), (0,)), ((), ())), preferred_element_type=F32)


def dot_nt(a, b):
    return lax.dot_general(a, b, (((1,), (1,)), ((), ())), preferred_element_type=F32)


def dot_tn(a, b):
    return lax.dot_general(a, b, (((0,), (0,)), ((), ())), preferred_element_type=F32)


def sigmoid(v):
    return 0.5 * jnp.tanh(0.5 * v) + 0.5


def block_diag(d, w):
    rows = []
    for j in range(d.group):
        parts = [w if i == j else jnp.zeros_like(w) for i in range(d.group)]
        rows.append(jnp.concatenate(parts, axis=1))
    return jnp.concatenate(rows, axis=0)


def permuted_rows(d, w):
    high = d.rank // d.group
    to = lax.broadcasted_iota(jnp.int32, (d.rank, d.rank), 0)
    at = lax.broadcasted_iota(jnp.int32, (d.rank, d.rank), 1)
    pick = (at == (to % high) * d.group + to // high).astype(F32).astype(BF)
    return dot(pick, w).astype(BF)


def head_rows(d, head, q, twice):
    row = lax.broadcasted_iota(jnp.int32, (d.lanes, d.channels), 0)
    wide = jnp.broadcast_to(head.astype(F32), (d.lanes, d.channels))
    parts = []
    for j in range(d.group):
        t = q * d.group + j
        hit = row == t
        if twice:
            hit = hit | (row == d.times + t)
        parts.append(jnp.where(hit, wide, 0.0))
    return jnp.concatenate(parts, axis=1).astype(BF)


def alive_mask(d, length):
    i = lax.broadcasted_iota(jnp.int32, (d.edge, d.width, d.lanes), 1)
    return (i < length * d.edge).reshape(d.rows, d.lanes)


def times_of(d, ref, q):
    return jnp.concatenate([ref[q * d.group + j] for j in range(d.group)], axis=1)


def diag_sum(d, total):
    out = None
    for j in range(d.group):
        part = total[j * d.rank : (j + 1) * d.rank, j * d.channels : (j + 1) * d.channels]
        out = part if out is None else out + part
    return out


def make_table(d, me, lengths, owner, tab):
    my_run = lax.fori_loop(0, d.nspace, lambda k, s: s + jnp.where(owner[k] == me, k, 0), jnp.int32(0))
    row = my_run // d.row_runs
    place = my_run % d.row_runs
    pair = row // 2
    start = jnp.int32(0)
    total = jnp.int32(0)
    for r in range(d.row_runs):
        one = lengths[pair, r]
        start = start + jnp.where(place > r, one, 0)
        total = total + one
    length = lengths[pair, place]
    row_count = d.nspace // d.row_runs
    tab[0] = length
    tab[1] = (place > 0).astype(jnp.int32)
    tab[2] = owner[jnp.maximum(my_run - 1, 0)]
    tab[3] = (place < d.row_runs - 1).astype(jnp.int32)
    tab[4] = owner[jnp.minimum(my_run + 1, d.nspace - 1)]
    for side, step in ((0, -1), (1, 1)):
        target = row + step
        valid = (target >= 0) & (target < row_count)
        there = jnp.clip(target, 0, row_count - 1)
        base = d.t_send + side * (1 + d.row_runs)
        tab[base] = valid.astype(jnp.int32)
        for r in range(d.row_runs):
            tab[base + 1 + r] = owner[there * d.row_runs + r]
        starts = []
        at = jnp.int32(0)
        for r in range(d.row_runs):
            starts.append(at)
            at = at + lengths[there // 2, r]
        for n in range(d.slots + 2):
            s = n - 1
            p = start + s
            ok = valid & (p >= 0) & (p < total) & (s <= length)
            run, first = jnp.int32(0), jnp.int32(0)
            for r in range(1, d.row_runs):
                past = starts[r] <= p
                run = jnp.where(past, r, run)
                first = jnp.where(past, starts[r], first)
            base = d.t_recv + (side * (d.slots + 2) + n) * 3
            tab[base] = ok.astype(jnp.int32)
            tab[base + 1] = owner[there * d.row_runs + run]
            tab[base + 2] = jnp.where(ok, p - first, 0)


def write_send(d, tab, own, send):
    for side, line in ((0, 0), (1, d.edge - 1)):
        base = d.t_send + side * (1 + d.row_runs)
        blocks = []
        for s in range(d.slots):
            at = line * d.width + s * d.edge
            blocks.append(
                jnp.concatenate([own[q, at : at + d.edge, :] for q in range(d.tiles)], axis=0).astype(BF)
            )

        @pl.when(tab[base] == 1)
        def _(base=base, blocks=blocks):
            for r in range(d.row_runs):
                for s in range(d.slots):
                    send[tab[base + 1 + r], s] = blocks[s]

    length = tab[0]
    for flag, to, at in ((1, 2, 0), (3, 4, length * d.edge - 1)):
        end = jnp.concatenate(
            [own[q, pl.ds(at, d.edge, stride=d.width), :] for q in range(d.tiles)], axis=0
        ).astype(BF)

        @pl.when(tab[flag] == 1)
        def _(to=to, end=end):
            send[tab[to], 0] = end


def fill(d, tab, own, recv, wide, shifted):
    length = tab[0]
    for q in range(d.tiles):
        wide[q] = jnp.zeros((d.span + 2 * SUB, d.lanes), F32)
        value = own[q].astype(F32)
        for c in range(d.edge):
            at = SUB + d.line * (c + 1)
            wide[q, at : at + d.width, :] = value[c * d.width : (c + 1) * d.width]
    first = SUB + d.line
    for flag, source, at in ((1, 2, first - 1), (3, 4, first + length * d.edge)):
        keep = tab[flag] == 1
        end = recv[tab[source], 0].astype(F32)
        end = jnp.where(keep, end, 0.0)
        for q in range(d.tiles):
            wide[q, pl.ds(at, d.edge, stride=d.line), :] = end[q * SUB : (q + 1) * SUB]
    sub = lax.broadcasted_iota(jnp.int32, (SUB, d.lanes), 0)
    for side, line in ((0, 0), (1, d.lines - 1)):
        at = SUB + d.line * line
        for n in range(d.slots + 2):
            s = n - 1
            base = d.t_recv + (side * (d.slots + 2) + n) * 3
            keep = tab[base] == 1
            value = recv[tab[base + 1], tab[base + 2]].astype(F32)
            value = jnp.where(keep, value, 0.0)
            for q in range(d.tiles):
                part = value[q * SUB : (q + 1) * SUB]
                if s < 0:
                    wide[q, at - 1 : at, :] = part[SUB - 1 : SUB]
                elif s == d.slots:
                    wide[q, at + s * SUB : at + s * SUB + 1, :] = part[0:1]
                else:
                    wide[q, at + s * SUB : (at + s * SUB) + SUB, :] = jnp.where((sub == 0) | (s < length), part, 0.0)
    for di in (-1, 0, 1):
        for q in range(d.tiles):
            shifted[di + 1, :, q * d.lanes : (q + 1) * d.lanes] = wide[
                q, SUB + di : SUB + di + d.span, :
            ].astype(BF)


def windows(d, shifted, direction, first, count):
    parts = []
    for di in (-1, 0, 1):
        for dc in (-1, 0, 1):
            at = d.line * (1 + direction * dc)
            parts.append(
                shifted[
                    1 + direction * di, at : at + d.core_rows, first * d.lanes : (first + count) * d.lanes
                ]
            )
    return parts


def convolve(d, shifted, inner, outer, direction, out):
    mul = dot if direction == 1 else dot_nt
    half = d.tiles // 2
    stacked = [
        jnp.concatenate(windows(d, shifted, direction, 2 * p, 2), axis=1) for p in range(half)
    ]
    total = mul(jnp.concatenate(stacked, axis=0), inner[...])
    for p in range(half):
        for n in range(2):
            out[2 * p + n] = total[p * d.core_rows : (p + 1) * d.core_rows, n * d.lanes : (n + 1) * d.lanes]
    for p in range(half - 1):
        total = mul(jnp.concatenate(windows(d, shifted, direction, 2 * p + 1, 2), axis=1), outer[...])
        for n in range(2):
            q = 2 * p + 1 + n
            out[q] = out[q] + total[:, n * d.lanes : (n + 1) * d.lanes]


def trimmed(d, value):
    return value.reshape(d.edge, d.line, d.lanes)[:, : d.width].reshape(d.rows, d.lanes)


def core_gradient(d, own, shifted, out):
    lane = lax.broadcasted_iota(jnp.int32, (1, d.lanes), 1) // d.rank
    tiles = []
    for q in range(d.tiles):
        value = own[q].astype(F32).reshape(d.edge, d.width, d.lanes)
        value = jnp.concatenate([value, jnp.zeros((d.edge, d.line - d.width, d.lanes), F32)], axis=1)
        tiles.append(value.reshape(d.core_rows, d.lanes))
    left = []
    zero = jnp.zeros_like(tiles[0])
    for q in range(d.tiles):
        after = tiles[q + 1] if q + 1 < d.tiles else zero
        before = tiles[q - 1] if q > 0 else zero
        mixed = jnp.where(lane == 0, after, jnp.where(lane == d.group - 1, before, 0.0))
        left.append(jnp.concatenate([tiles[q], mixed], axis=1).astype(BF))
    left = jnp.concatenate(left, axis=0)
    rank, group = d.rank, d.group
    high = rank // group
    wide_lane = lax.broadcasted_iota(jnp.int32, (high, d.lanes), 1) // rank
    for k in range(d.taps):
        right = jnp.concatenate([windows(d, shifted, -1, q, 1)[k] for q in range(d.tiles)], axis=0)
        total = dot_tn(left, right)
        for dt in (-1, 0, 1):
            pieces = []
            for j in range(group):
                if 0 <= j + dt < group:
                    at = (j + dt) * rank
                elif j + dt == group:
                    at = d.lanes
                else:
                    at = d.lanes + (group - 1) * rank
                pieces.append(total[at : at + rank])
            result = None
            for turn in range(group):
                mix = None
                for j in range(group):
                    rl = (j + turn) % group
                    part = pieces[j][rl * high : (rl + 1) * high]
                    mix = part if mix is None else jnp.where(wide_lane == j, part, mix)
                if turn:
                    mix = pltpu.roll(mix, turn * rank, 1)
                result = mix if result is None else result + mix
            o = 3 * k + dt + 1
            out[o * high : (o + 1) * high, :] = result


def bands_kernel(d, core_ref, inner_ref, outer_ref, inner_t_ref, outer_t_ref, flat):
    rank, group, lanes = d.rank, d.group, d.lanes
    high = rank // group
    for rh in range(high):
        flat[pl.ds(rh, 27, stride=high), :] = core_ref[:, rh * lanes : (rh + 1) * lanes].astype(F32)
    rows = flat[...].astype(BF)
    at = lax.broadcasted_iota(jnp.int32, (lanes, lanes), 0)
    to = lax.broadcasted_iota(jnp.int32, (lanes, lanes), 1)
    spread = []
    for rl in range(group):
        pick = (at == rl * rank + to % rank).astype(F32).astype(BF)
        spread.append(dot(rows, pick))
    lane = lax.broadcasted_iota(jnp.int32, (rank, lanes), 1) // rank
    zero = jnp.zeros((rank, lanes), BF)
    size = 2 * lanes
    for k in range(d.taps):
        full = []
        for dt in (-1, 0, 1):
            o = 3 * k + dt + 1
            full.append(
                jnp.concatenate([spread[rl][o * high : (o + 1) * high] for rl in range(group)], axis=0)
            )
        cache = {}
        for delta in range(-1, group + 1):
            value = jnp.zeros((rank, lanes), F32)
            for dt in (-1, 0, 1):
                value = jnp.where(lane == delta - dt, full[dt + 1], value)
            cache[delta] = value.astype(BF)

        def put(down, across, value, inside):
            one, two = (inner_ref, inner_t_ref) if inside else (outer_ref, outer_t_ref)
            one[k * size + down * rank : k * size + (down + 1) * rank, across * lanes : (across + 1) * lanes] = value
            two[down * rank : (down + 1) * rank, k * size + across * lanes : k * size + (across + 1) * lanes] = value

        for down in range(2 * group):
            for across in range(2):
                put(down, across, cache.get(down - across * group, zero), True)
                value = zero
                if down == group - 1 and across == 1:
                    value = cache[-1]
                if down == group and across == 0:
                    value = cache[group]
                put(down, across, value, False)


def first_kernel(d, me, lengths, owner, x_hbm, reduce_ref, tab, xt, own_out, send, xc, xf, own, sems):
    copies = []
    for c in range(d.edge):
        copies.append(pltpu.make_async_copy(x_hbm.at[:, :, c], xc.at[c], sems.at[c]))
    for copy in copies:
        copy.start()
    make_table(d, me[0], lengths, owner, tab)
    weight = block_diag(d, permuted_rows(d, reduce_ref[...]))
    per_line = d.width * d.times
    for c, copy in enumerate(copies):
        copy.wait()
        xf[c * per_line : (c + 1) * per_line, :] = xc[c].reshape(per_line, d.channels).astype(F32)
    alive = alive_mask(d, tab[0])
    for q in range(d.tiles):
        for j in range(d.group):
            t = q * d.group + j
            xt[t] = xf[pl.ds(t, d.rows, stride=d.times), :].astype(BF)
        value = dot_nt(times_of(d, xt, q), weight)
        value = jnp.where(alive, value, 0.0).astype(BF)
        own_out[q] = value
        own[q] = value.astype(F32)
    write_send(d, tab, own, send)


def layer_one_kernel(
    d, tab, own_in, recv, inner, outer, expand_ref, reduce_next, source, mixed, hidden, own_out, send,
    wide, shifted, conv, own,
):
    fill(d, tab, own_in, recv, wide, shifted)
    convolve(d, shifted, inner, outer, 1, conv)
    expand = block_diag(d, expand_ref[...])
    weight = block_diag(d, permuted_rows(d, reduce_next[...]))
    alive = alive_mask(d, tab[0])
    for q in range(d.tiles):
        b = trimmed(d, conv[q]).astype(BF)
        mixed[q] = b
        y = dot(b, expand)
        for j in range(d.group):
            t = q * d.group + j
            v = y[:, j * d.channels : (j + 1) * d.channels]
            hidden[t] = (source[t].astype(F32) + v * sigmoid(v)).astype(BF)
        value = dot_nt(times_of(d, hidden, q), weight)
        value = jnp.where(alive, value, 0.0).astype(BF)
        own_out[q] = value
        own[q] = value.astype(F32)
    write_send(d, tab, own, send)


def layer_two_kernel(
    d, tab, own_in, recv, inner, outer, expand_ref, head_ref, source, labels, own_out, send, chance_out, g_out,
    expand_grad, head_grad, wide, shifted, conv, own, slope, last, mixed,
):
    fill(d, tab, own_in, recv, wide, shifted)
    convolve(d, shifted, inner, outer, 1, conv)
    expand = block_diag(d, expand_ref[...])
    head = head_ref[...]
    logit = jnp.zeros((d.rows, d.lanes), F32)
    for q in range(d.tiles):
        b = trimmed(d, conv[q]).astype(BF)
        mixed[q] = b
        y = dot(b, expand)
        for j in range(d.group):
            t = q * d.group + j
            v = y[:, j * d.channels : (j + 1) * d.channels]
            s = sigmoid(v)
            slope[t] = s * (1.0 + v * (1.0 - s))
            last[t] = (source[t].astype(F32) + v * s).astype(BF)
        logit = logit + dot_nt(times_of(d, last, q), head_rows(d, head, q, False))
    chance = jax.nn.sigmoid(logit)
    lane = lax.broadcasted_iota(jnp.int32, (d.rows, d.lanes), 1)
    live = alive_mask(d, tab[0]) & (lane < d.times)
    chance = jnp.where(live, chance, 0.0)
    chance_out[...] = chance
    g = jnp.where(live, chance - labels[...], 0.0)
    coarse = g.astype(BF).astype(F32)
    pair = (coarse + pltpu.roll(g - coarse, d.times, 1)).astype(BF)
    g_out[...] = pair
    grad_e = jnp.zeros((d.rank, d.channels), F32)
    grad_h = jnp.zeros((1, d.channels), F32)
    for q in range(d.tiles):
        up = dot(pair, head_rows(d, head, q, True))
        delta = jnp.concatenate(
            [
                up[:, j * d.channels : (j + 1) * d.channels] * slope[q * d.group + j]
                for j in range(d.group)
            ],
            axis=1,
        ).astype(BF)
        value = dot_nt(delta, expand).astype(BF)
        own_out[q] = value
        own[q] = value.astype(F32)
        grad_e = grad_e + diag_sum(d, dot_tn(mixed[q], delta))
        total = dot_tn(pair, times_of(d, last, q))
        for j in range(d.group):
            t = q * d.group + j
            at = slice(j * d.channels, (j + 1) * d.channels)
            grad_h = grad_h + total[t : t + 1, at] + total[d.times + t : d.times + t + 1, at]
    expand_grad[...] = grad_e
    head_grad[...] = jnp.concatenate([grad_h, jnp.zeros((SUB - 1, d.channels), F32)], axis=0)
    write_send(d, tab, own, send)


def back_two_kernel(
    d, tab, own_in, recv, inner_t, outer_t, reduce_ref, expand_ref, head_ref, source, mixed, g_in,
    own_out, send, reduce_grad, expand_grad, shifted, wide, conv, own,
):
    fill(d, tab, own_in, recv, wide, shifted)
    convolve(d, shifted, inner_t, outer_t, -1, conv)
    expand = block_diag(d, expand_ref[...])
    weight = block_diag(d, permuted_rows(d, reduce_ref[...]))
    head = head_ref[...]
    alive = alive_mask(d, tab[0])
    pair = g_in[...]
    grad_r = jnp.zeros((d.rank, d.channels), F32)
    grad_e = jnp.zeros((d.rank, d.channels), F32)
    for q in range(d.tiles):
        da = jnp.where(alive, trimmed(d, conv[q]), 0.0).astype(BF)
        grad_r = grad_r + diag_sum(d, dot_tn(da, times_of(d, source, q)))
        up = dot(
            jnp.concatenate([da, pair], axis=1),
            jnp.concatenate([weight, head_rows(d, head, q, True)], axis=0),
        )
        b = mixed[q]
        y = dot(b, expand)
        parts = []
        for j in range(d.group):
            at = slice(j * d.channels, (j + 1) * d.channels)
            v = y[:, at]
            s = sigmoid(v)
            parts.append((up[:, at] * (s * (1.0 + v * (1.0 - s)))).astype(BF))
        delta = jnp.concatenate(parts, axis=1)
        value = dot_nt(delta, expand).astype(BF)
        own_out[q] = value
        own[q] = value.astype(F32)
        grad_e = grad_e + diag_sum(d, dot_tn(b, delta))
    reduce_grad[...] = grad_r
    expand_grad[...] = grad_e
    write_send(d, tab, own, send)


def core_kernel(d, own, shifted, out):
    core_gradient(d, own, shifted, out)


def back_one_kernel(
    d, tab, own_in, recv, inner_t, outer_t, own_first, source, core_two, expand_one, reduce_two, expand_two, head,
    packed, wide, shifted, conv,
):
    fill(d, tab, own_in, recv, wide, shifted)
    convolve(d, shifted, inner_t, outer_t, -1, conv)
    alive = alive_mask(d, tab[0])
    grad_r = jnp.zeros((d.rank, d.channels), F32)
    for q in range(d.tiles):
        da = jnp.where(alive, trimmed(d, conv[q]), 0.0).astype(BF)
        grad_r = grad_r + diag_sum(d, dot_tn(da, times_of(d, source, q)))
    off = d.offsets
    core_gradient(d, own_first, shifted, packed)
    packed[off[1] : off[2], :] = core_two[...]
    packed[off[2] : off[3], :] = grad_r
    packed[off[3] : off[4], :] = expand_one[...]
    packed[off[4] : off[5], :] = reduce_two[...]
    packed[off[5] : off[6], :] = expand_two[...]
    packed[off[6] : off[7], :] = head[...]
    rest = d.nspace * d.share - off[7]
    if rest:
        packed[off[7] :, :] = jnp.zeros((rest, d.channels), F32)


def sum_kernel(d, parts, out):
    total = parts[0]
    for n in range(1, d.nspace):
        total = total + parts[n]
    total = total * (1.0 / d.cells)
    for n in range(d.nspace):
        out[n] = total


def unpack_kernel(d, packed, reduce_one, core_one, expand_one, reduce_two, core_two, expand_two, head):
    off = d.offsets
    high = d.rank // d.group
    for at, core in ((off[0], core_one), (off[1], core_two)):
        for rh in range(high):
            core[:, rh * d.lanes : (rh + 1) * d.lanes] = packed[pl.ds(at + rh, 27, stride=high), :]
    for at, ref in ((off[2], reduce_one), (off[4], reduce_two)):
        for rl in range(d.group):
            ref[pl.ds(rl, high, stride=d.group), :] = packed[at + rl * high : at + (rl + 1) * high, :]
    expand_one[...] = packed[off[3] : off[4], :]
    expand_two[...] = packed[off[5] : off[6], :]
    head[...] = packed[off[6] : off[6] + 1, :]


VM = pl.BlockSpec(memory_space=pltpu.VMEM)
SM = pl.BlockSpec(memory_space=pltpu.SMEM)
HB = pl.BlockSpec(memory_space=pl.ANY)


def call(kernel, d, name, ins, outs, scratch, operands):
    shapes = tuple(jax.ShapeDtypeStruct(s, t) for s, t, _ in outs)
    specs = tuple(m for _, _, m in outs)
    return pl.pallas_call(
        functools.partial(kernel, d),
        out_shape=shapes,
        in_specs=list(ins),
        out_specs=specs,
        scratch_shapes=scratch,
        name=name,
        compiler_params=pltpu.CompilerParams(vmem_limit_bytes=LIMIT),
    )(*operands)


def on_device(
    volume, labels, run_lengths, run_owner, reduce_one, core_one, expand_one, reduce_two, core_two, expand_two,
    head_vector,
):
    nspace = lax.axis_size("space")
    slots, edge, _, times, channels = volume.shape
    rank = reduce_one.shape[0]
    d = Dims(nspace, slots, edge, times, channels, rank, run_lengths.shape[0], run_lengths.shape[1])
    me = lax.axis_index("space").astype(jnp.int32).reshape(1)
    head = head_vector.reshape(1, channels)
    targets = labels.reshape(slots, edge, edge, times).transpose(2, 0, 1, 3).reshape(d.rows, times)
    targets = jnp.pad(targets.astype(F32), ((0, 0), (0, d.lanes - times)))

    own_shape = (d.tiles, d.rows, d.lanes)
    wide_shape = (d.times, d.rows, d.channels)
    send_shape = (nspace,) + d.block
    shifted_shape = (3, d.span, d.tiles * d.lanes)
    own_f = pltpu.VMEM(own_shape, F32)
    rim = pltpu.VMEM((d.tiles, d.span + 2 * SUB, d.lanes), F32)
    shifted = pltpu.VMEM(shifted_shape, BF)
    conv = pltpu.VMEM((d.tiles, d.core_rows, d.lanes), F32)
    small = ((rank, channels), F32, VM)
    size = 2 * d.lanes

    def exchange(send):
        return lax.all_to_all(send, "space", split_axis=0, concat_axis=0, tiled=True)

    def bands(core, name):
        return call(
            bands_kernel, d, name, [VM],
            [((9 * size, size), BF, VM)] * 2 + [((size, 9 * size), BF, VM)] * 2,
            [pltpu.VMEM((27 * rank // d.group, d.lanes), F32)], [core],
        )

    tab, xt, a1, send = call(
        first_kernel, d, "first", [SM, SM, SM, HB, VM],
        [((d.t_size,), jnp.int32, SM), (wide_shape, BF, VM), (own_shape, BF, VM), (send_shape, BF, VM)],
        [
            pltpu.VMEM((edge, slots, edge, times, channels), BF),
            pltpu.VMEM((d.rows * times, channels), F32),
            own_f,
            pltpu.SemaphoreType.DMA((edge,)),
        ],
        [me, run_lengths, run_owner, volume, reduce_one],
    )
    inner1, outer1, inner1t, outer1t = bands(core_one, "bands_one")
    inner2, outer2, inner2t, outer2t = bands(core_two, "bands_two")
    recv = exchange(send)
    b1, h1, a2, send = call(
        layer_one_kernel, d, "layer_one", [SM] + [VM] * 7,
        [(own_shape, BF, VM), (wide_shape, BF, VM), (own_shape, BF, VM), (send_shape, BF, VM)],
        [rim, shifted, conv, own_f],
        [tab, a1, recv, inner1, outer1, expand_one, reduce_two, xt],
    )
    recv = exchange(send)
    db2, send, chance, g, eg2, hg = call(
        layer_two_kernel, d, "layer_two", [SM] + [VM] * 8,
        [
            (own_shape, BF, VM), (send_shape, BF, VM), ((d.rows, d.lanes), F32, VM), ((d.rows, d.lanes), BF, VM),
            small, ((SUB, channels), F32, VM),
        ],
        [rim, shifted, conv, own_f, pltpu.VMEM(wide_shape, F32), pltpu.VMEM(wide_shape, BF), pltpu.VMEM(own_shape, BF)],
        [tab, a2, recv, inner2, outer2, expand_two, head, h1, targets],
    )
    recv = exchange(send)
    db1, send, rg2, eg1, around = call(
        back_two_kernel, d, "back_two", [SM] + [VM] * 10,
        [(own_shape, BF, VM), (send_shape, BF, VM), small, small, (shifted_shape, BF, VM)],
        [rim, conv, own_f],
        [tab, db2, recv, inner2t, outer2t, reduce_two, expand_one, head, h1, b1, g],
    )
    core_shape = (27 * rank // d.group, d.lanes)
    (cg2,) = call(core_kernel, d, "core_two", [VM] * 2, [(core_shape, F32, VM)], [], [a2, around])
    recv = exchange(send)
    (packed,) = call(
        back_one_kernel, d, "back_one", [SM] + [VM] * 11,
        [((nspace * d.share, channels), F32, VM)],
        [rim, shifted, conv],
        [tab, db1, recv, inner1t, outer1t, a1, xt, cg2, eg1, rg2, eg2, hg],
    )
    parts = exchange(packed.reshape(nspace, d.share, channels))
    (sums,) = call(
        sum_kernel, d, "sum_parts", [VM], [((nspace, d.share, channels), F32, VM)], [], [parts]
    )
    whole = exchange(sums).reshape(nspace * d.share, channels)
    core_out = ((27, rank * rank), F32, VM)
    r1, c1, e1, r2, c2, e2, hv = call(
        unpack_kernel, d, "unpack", [VM],
        [small, core_out, small, small, core_out, small, ((1, channels), F32, VM)], [], [whole],
    )
    prob = chance[:, :times].reshape(edge, slots, edge, times).transpose(1, 2, 0, 3).reshape(slots, -1)
    return prob, r1, c1, e1, r2, c2, e2, hv.reshape(channels)


def solution(mesh):
    in_specs = (
        P(("groups", "space"), None, None, None, None),
        P(("groups", "space"), None),
        P("groups", None),
        P("groups"),
    ) + (P(),) * 7
    out_specs = (P(("groups", "space"), None),) + (P("groups", None),) * 6 + (P("groups"),)
    return jax.shard_map(on_device, mesh=mesh, in_specs=in_specs, out_specs=out_specs, check_vma=False)
```

```python
import functools

import jax
import jax.numpy as jnp
from jax import lax
from jax.experimental import pallas as pl
from jax.experimental.pallas import tpu as pltpu
from jax.sharding import PartitionSpec as P

BF = jnp.bfloat16
F32 = jnp.float32
SUB = 8
LIMIT = 24 * 1024 * 1024


class Dims:
    def __init__(self, nspace, slots, edge, times, channels, rank, pairs, row_runs):
        self.nspace, self.slots, self.edge, self.times = nspace, slots, edge, times
        self.channels, self.rank, self.pairs, self.row_runs = channels, rank, pairs, row_runs
        self.lanes = channels
        self.group = channels // rank
        self.tiles = times // self.group
        self.width = slots * edge
        self.rows = edge * self.width
        self.line = self.width + SUB
        self.lines = edge + 2
        self.span = self.lines * self.line
        self.core_rows = edge * self.line
        self.cells = edge * edge * times
        self.taps = 9
        self.t_send = 5
        self.t_recv = self.t_send + 2 * (1 + row_runs)
        self.t_size = self.t_recv + 2 * 3 * (slots + 2)
        self.part = self.tiles * SUB
        self.block = slots * self.part
        per_row = rank * rank // channels
        sizes = [27 * per_row, 27 * per_row, rank, rank, rank, SUB]
        self.offsets = [sum(sizes[:i]) for i in range(len(sizes) + 1)]
        self.share = -(-self.offsets[-1] // (nspace * SUB)) * SUB


def dot(a, b):
    return lax.dot_general(a, b, (((1,), (0,)), ((), ())), preferred_element_type=F32)


def dot_nt(a, b):
    return lax.dot_general(a, b, (((1,), (1,)), ((), ())), preferred_element_type=F32)


def dot_tn(a, b):
    return lax.dot_general(a, b, (((0,), (0,)), ((), ())), preferred_element_type=F32)


def sigmoid(v):
    return 0.5 * jnp.tanh(0.5 * v) + 0.5


def block_diag(d, w):
    rows = []
    for j in range(d.group):
        parts = [w if i == j else jnp.zeros_like(w) for i in range(d.group)]
        rows.append(jnp.concatenate(parts, axis=1))
    return jnp.concatenate(rows, axis=0)


def permuted_rows(d, w):
    high = d.rank // d.group
    to = lax.broadcasted_iota(jnp.int32, (d.rank, d.rank), 0)
    at = lax.broadcasted_iota(jnp.int32, (d.rank, d.rank), 1)
    pick = (at == (to % high) * d.group + to // high).astype(F32).astype(BF)
    return dot(pick, w).astype(BF)


def head_rows(d, head, q, twice):
    row = lax.broadcasted_iota(jnp.int32, (d.lanes, d.channels), 0)
    wide = jnp.broadcast_to(head.astype(F32), (d.lanes, d.channels))
    parts = []
    for j in range(d.group):
        t = q * d.group + j
        hit = row == t
        if twice:
            hit = hit | (row == d.times + t)
        parts.append(jnp.where(hit, wide, 0.0))
    return jnp.concatenate(parts, axis=1).astype(BF)


def alive_mask(d, length):
    i = lax.broadcasted_iota(jnp.int32, (d.edge, d.width, d.lanes), 1)
    return (i < length * d.edge).reshape(d.rows, d.lanes)


def times_of(d, ref, q):
    return jnp.concatenate([ref[q * d.group + j] for j in range(d.group)], axis=1)


def diag_sum(d, total):
    out = None
    for j in range(d.group):
        part = total[j * d.rank : (j + 1) * d.rank, j * d.channels : (j + 1) * d.channels]
        out = part if out is None else out + part
    return out


def make_table(d, me, lengths, owner, tab):
    my_run = lax.fori_loop(0, d.nspace, lambda k, s: s + jnp.where(owner[k] == me, k, 0), jnp.int32(0))
    row = my_run // d.row_runs
    place = my_run % d.row_runs
    pair = row // 2
    start = jnp.int32(0)
    total = jnp.int32(0)
    for r in range(d.row_runs):
        one = lengths[pair, r]
        start = start + jnp.where(place > r, one, 0)
        total = total + one
    length = lengths[pair, place]
    row_count = d.nspace // d.row_runs
    tab[0] = length
    tab[1] = (place > 0).astype(jnp.int32)
    tab[2] = owner[jnp.maximum(my_run - 1, 0)]
    tab[3] = (place < d.row_runs - 1).astype(jnp.int32)
    tab[4] = owner[jnp.minimum(my_run + 1, d.nspace - 1)]
    for side, step in ((0, -1), (1, 1)):
        target = row + step
        valid = (target >= 0) & (target < row_count)
        there = jnp.clip(target, 0, row_count - 1)
        base = d.t_send + side * (1 + d.row_runs)
        tab[base] = valid.astype(jnp.int32)
        for r in range(d.row_runs):
            tab[base + 1 + r] = owner[there * d.row_runs + r]
        starts = []
        at = jnp.int32(0)
        for r in range(d.row_runs):
            starts.append(at)
            at = at + lengths[there // 2, r]
        for n in range(d.slots + 2):
            s = n - 1
            p = start + s
            ok = valid & (p >= 0) & (p < total) & (s <= length)
            run, first = jnp.int32(0), jnp.int32(0)
            for r in range(1, d.row_runs):
                past = starts[r] <= p
                run = jnp.where(past, r, run)
                first = jnp.where(past, starts[r], first)
            base = d.t_recv + (side * (d.slots + 2) + n) * 3
            tab[base] = ok.astype(jnp.int32)
            tab[base + 1] = owner[there * d.row_runs + run]
            tab[base + 2] = jnp.where(ok, p - first, 0)


def write_send(d, tab, own, send):
    for side, line in ((0, 0), (1, d.edge - 1)):
        base = d.t_send + side * (1 + d.row_runs)
        blocks = []
        for s in range(d.slots):
            at = line * d.width + s * d.edge
            blocks.append(
                jnp.concatenate([own[q, at : at + d.edge, :] for q in range(d.tiles)], axis=0).astype(BF)
            )

        @pl.when(tab[base] == 1)
        def _(base=base, blocks=blocks):
            for r in range(d.row_runs):
                for s in range(d.slots):
                    send[tab[base + 1 + r], s * d.part : (s + 1) * d.part, :] = blocks[s]

    length = tab[0]
    for flag, to, at in ((1, 2, 0), (3, 4, length * d.edge - 1)):
        end = jnp.concatenate(
            [own[q, pl.ds(at, d.edge, stride=d.width), :] for q in range(d.tiles)], axis=0
        ).astype(BF)

        @pl.when(tab[flag] == 1)
        def _(to=to, end=end):
            send[tab[to], : d.part, :] = end


def fill(d, tab, own, recv, wide, shifted):
    length = tab[0]
    for q in range(d.tiles):
        wide[q] = jnp.zeros((d.span + 2 * SUB, d.lanes), F32)
        value = own[q].astype(F32)
        for c in range(d.edge):
            at = SUB + d.line * (c + 1)
            wide[q, at : at + d.width, :] = value[c * d.width : (c + 1) * d.width]
    first = SUB + d.line
    for flag, source, at in ((1, 2, first - 1), (3, 4, first + length * d.edge)):
        keep = tab[flag] == 1
        end = recv[tab[source], : d.part, :].astype(F32)
        end = jnp.where(keep, end, 0.0)
        for q in range(d.tiles):
            wide[q, pl.ds(at, d.edge, stride=d.line), :] = end[q * SUB : (q + 1) * SUB]
    sub = lax.broadcasted_iota(jnp.int32, (SUB, d.lanes), 0)
    for side, line in ((0, 0), (1, d.lines - 1)):
        at = SUB + d.line * line
        for n in range(d.slots + 2):
            s = n - 1
            base = d.t_recv + (side * (d.slots + 2) + n) * 3
            keep = tab[base] == 1
            value = recv[tab[base + 1], pl.ds(pl.multiple_of(tab[base + 2] * d.part, d.part), d.part), :]
            value = jnp.where(keep, value.astype(F32), 0.0)
            for q in range(d.tiles):
                part = value[q * SUB : (q + 1) * SUB]
                if s < 0:
                    wide[q, at - 1 : at, :] = part[SUB - 1 : SUB]
                elif s == d.slots:
                    wide[q, at + s * SUB : at + s * SUB + 1, :] = part[0:1]
                else:
                    wide[q, at + s * SUB : (at + s * SUB) + SUB, :] = jnp.where((sub == 0) | (s < length), part, 0.0)
    for di in (-1, 0, 1):
        for q in range(d.tiles):
            shifted[di + 1, :, q * d.lanes : (q + 1) * d.lanes] = wide[
                q, SUB + di : SUB + di + d.span, :
            ].astype(BF)


def windows(d, shifted, direction, first, count):
    parts = []
    for di in (-1, 0, 1):
        for dc in (-1, 0, 1):
            at = d.line * (1 + direction * dc)
            parts.append(
                shifted[
                    1 + direction * di, at : at + d.core_rows, first * d.lanes : (first + count) * d.lanes
                ]
            )
    return parts


def bands(d, core, flat, inner, outer, across_taps):
    rank, group, lanes = d.rank, d.group, d.lanes
    high = rank // group
    for rh in range(high):
        flat[pl.ds(rh, 27, stride=high), :] = core[:, rh * lanes : (rh + 1) * lanes].astype(F32)
    rows = flat[...].astype(BF)
    at = lax.broadcasted_iota(jnp.int32, (lanes, lanes), 0)
    to = lax.broadcasted_iota(jnp.int32, (lanes, lanes), 1)
    spread = []
    for rl in range(group):
        pick = (at == rl * rank + to % rank).astype(F32).astype(BF)
        spread.append(dot(rows, pick))
    lane = lax.broadcasted_iota(jnp.int32, (rank, lanes), 1) // rank
    zero = jnp.zeros((rank, lanes), BF)
    size = 2 * lanes
    for k in range(d.taps):
        full = []
        for dt in (-1, 0, 1):
            o = 3 * k + dt + 1
            full.append(
                jnp.concatenate([spread[rl][o * high : (o + 1) * high] for rl in range(group)], axis=0)
            )
        cache = {}
        for delta in range(-1, group + 1):
            value = jnp.zeros((rank, lanes), F32)
            for dt in (-1, 0, 1):
                value = jnp.where(lane == delta - dt, full[dt + 1], value)
            cache[delta] = value.astype(BF)
        down0, across0 = (0, k * size) if across_taps else (k * size, 0)
        for down in range(2 * group):
            for across in range(2):
                value = zero
                if down == group - 1 and across == 1:
                    value = cache[-1]
                if down == group and across == 0:
                    value = cache[group]
                row = slice(down0 + down * rank, down0 + (down + 1) * rank)
                col = slice(across0 + across * lanes, across0 + (across + 1) * lanes)
                inner[row, col] = cache.get(down - across * group, zero)
                outer[row, col] = value


def convolve(d, shifted, inner, outer, direction, out):
    mul = dot if direction == 1 else dot_nt
    half = d.tiles // 2
    stacked = [
        jnp.concatenate(windows(d, shifted, direction, 2 * p, 2), axis=1) for p in range(half)
    ]
    total = mul(jnp.concatenate(stacked, axis=0), inner[...])
    for p in range(half):
        for n in range(2):
            out[2 * p + n] = total[p * d.core_rows : (p + 1) * d.core_rows, n * d.lanes : (n + 1) * d.lanes]
    for p in range(half - 1):
        total = mul(jnp.concatenate(windows(d, shifted, direction, 2 * p + 1, 2), axis=1), outer[...])
        for n in range(2):
            q = 2 * p + 1 + n
            out[q] = out[q] + total[:, n * d.lanes : (n + 1) * d.lanes]


def trimmed(d, value):
    return value.reshape(d.edge, d.line, d.lanes)[:, : d.width].reshape(d.rows, d.lanes)


def core_gradient(d, shifted, own, out):
    lane = lax.broadcasted_iota(jnp.int32, (1, d.lanes), 1) // d.rank
    tiles = []
    for q in range(d.tiles):
        value = own[q].astype(F32).reshape(d.edge, d.width, d.lanes)
        value = jnp.concatenate([value, jnp.zeros((d.edge, d.line - d.width, d.lanes), F32)], axis=1)
        tiles.append(value.reshape(d.core_rows, d.lanes))
    right = []
    zero = jnp.zeros_like(tiles[0])
    for q in range(d.tiles):
        after = tiles[q + 1] if q + 1 < d.tiles else zero
        before = tiles[q - 1] if q > 0 else zero
        mixed = jnp.where(lane == 0, after, jnp.where(lane == d.group - 1, before, 0.0))
        right.append(jnp.concatenate([tiles[q], mixed], axis=1).astype(BF))
    right = jnp.concatenate(right, axis=0)
    rank, group = d.rank, d.group
    high = rank // group
    wide_lane = lax.broadcasted_iota(jnp.int32, (high, d.lanes), 1) // rank
    for k in range(d.taps):
        left = jnp.concatenate([windows(d, shifted, 1, q, 1)[k] for q in range(d.tiles)], axis=0)
        total = dot_tn(left, right)
        for dt in (-1, 0, 1):
            pieces = []
            for j in range(group):
                if 0 <= j + dt < group:
                    row, col = j + dt, 0
                elif j + dt == group:
                    row, col = 0, 1
                else:
                    row, col = group - 1, 1
                pieces.append(total[row * rank : (row + 1) * rank, col * d.lanes : (col + 1) * d.lanes])
            result = None
            for turn in range(group):
                mix = None
                for j in range(group):
                    rl = (j + turn) % group
                    part = pieces[j][rl * high : (rl + 1) * high]
                    mix = part if mix is None else jnp.where(wide_lane == j, part, mix)
                if turn:
                    mix = pltpu.roll(mix, turn * rank, 1)
                result = mix if result is None else result + mix
            o = 3 * k + dt + 1
            out[o * high : (o + 1) * high, :] = result


class Copies:
    def __init__(self, sems, pairs):
        self.all = [pltpu.make_async_copy(a, b, sems.at[n]) for n, (a, b) in enumerate(pairs)]
        for one in self.all:
            one.start()

    def wait(self, *which):
        for n in which:
            self.all[n].wait()


def first_kernel(
    d, me, lengths_hbm, owner_hbm, x_hbm, reduce_hbm, tab_out, xt, own_out, send, xc, xf, own, reduce_ref, lengths, owner,
    tab, sems,
):
    e = d.edge
    copies = Copies(
        sems,
        [(lengths_hbm, lengths), (owner_hbm, owner)]
        + [(x_hbm.at[:, :, c], xc.at[c]) for c in range(e)]
        + [(reduce_hbm, reduce_ref)],
    )
    copies.wait(0, 1)
    make_table(d, me[0], lengths, owner, tab)
    save = pltpu.make_async_copy(tab, tab_out, sems.at[e + 3])
    save.start()
    copies.wait(e + 2)
    weight = block_diag(d, permuted_rows(d, reduce_ref[...]))
    per_line = d.width * d.times
    for c in range(e):
        copies.wait(2 + c)
        xf[c * per_line : (c + 1) * per_line, :] = xc[c].reshape(per_line, d.channels).astype(F32)
    alive = alive_mask(d, tab[0])
    for q in range(d.tiles):
        for j in range(d.group):
            t = q * d.group + j
            xt[t] = xf[pl.ds(t, d.rows, stride=d.times), :].astype(BF)
        value = dot_nt(times_of(d, xt, q), weight)
        value = jnp.where(alive, value, 0.0).astype(BF)
        own_out[q] = value
        own[q] = value.astype(F32)
    write_send(d, tab, own, send)
    save.wait()


def layer_one_kernel(
    d, tab_in, own_in, recv, core_hbm, expand_hbm, reduce_hbm, source, mixed, hidden, own_out, send, around,
    wide, shifted, conv, own, flat, inner, outer, core, expand_ref, reduce_next, tab, sems,
):
    copies = Copies(
        sems, [(tab_in, tab), (core_hbm, core), (expand_hbm, expand_ref), (reduce_hbm, reduce_next)]
    )
    copies.wait(0)
    fill(d, tab, own_in, recv, wide, shifted)
    save = pltpu.make_async_copy(shifted, around, sems.at[4])
    save.start()
    copies.wait(1, 2, 3)
    bands(d, core, flat, inner, outer, False)
    convolve(d, shifted, inner, outer, 1, conv)
    expand = block_diag(d, expand_ref[...])
    weight = block_diag(d, permuted_rows(d, reduce_next[...]))
    alive = alive_mask(d, tab[0])
    for q in range(d.tiles):
        b = trimmed(d, conv[q]).astype(BF)
        mixed[q] = b
        y = dot(b, expand)
        for j in range(d.group):
            t = q * d.group + j
            v = y[:, j * d.channels : (j + 1) * d.channels]
            hidden[t] = (source[t].astype(F32) + v * sigmoid(v)).astype(BF)
        value = dot_nt(times_of(d, hidden, q), weight)
        value = jnp.where(alive, value, 0.0).astype(BF)
        own_out[q] = value
        own[q] = value.astype(F32)
    write_send(d, tab, own, send)
    save.wait()


def read_labels(d, labels, plane):
    for i in range(d.edge):
        part = labels[:, i * d.lanes : (i + 1) * d.lanes].astype(F32)
        plane[pl.ds(i, d.slots, stride=d.edge), :] = part
    value = plane[...]
    lines = [value if c == 0 else pltpu.roll(value, d.lanes - c * d.times, 1) for c in range(d.edge)]
    return jnp.concatenate(lines, axis=0)


def write_prob(d, chance, plane, prob):
    total = chance[: d.width]
    for c in range(1, d.edge):
        total = total + pltpu.roll(chance[c * d.width : (c + 1) * d.width], c * d.times, 1)
    plane[...] = total
    for i in range(d.edge):
        prob[:, i * d.lanes : (i + 1) * d.lanes] = plane[pl.ds(i, d.slots, stride=d.edge), :]


def layer_two_kernel(
    d, tab_in, own_in, recv, core_hbm, expand_hbm, head_hbm, source, labels_hbm, own_out, send, prob, g_out,
    expand_grad, head_grad, around, wide, shifted, conv, own, slope, last, mixed, flat, inner, outer, core,
    expand_ref, head_ref, labels, plane, tab, sems,
):
    copies = Copies(
        sems,
        [(tab_in, tab), (core_hbm, core), (expand_hbm, expand_ref), (head_hbm, head_ref), (labels_hbm, labels)],
    )
    copies.wait(0)
    fill(d, tab, own_in, recv, wide, shifted)
    save = pltpu.make_async_copy(shifted, around, sems.at[5])
    save.start()
    copies.wait(1, 2, 3, 4)
    bands(d, core, flat, inner, outer, False)
    convolve(d, shifted, inner, outer, 1, conv)
    expand = block_diag(d, expand_ref[...])
    head = head_ref[...]
    logit = jnp.zeros((d.rows, d.lanes), F32)
    for q in range(d.tiles):
        b = trimmed(d, conv[q]).astype(BF)
        mixed[q] = b
        y = dot(b, expand)
        for j in range(d.group):
            t = q * d.group + j
            v = y[:, j * d.channels : (j + 1) * d.channels]
            s = sigmoid(v)
            slope[t] = s * (1.0 + v * (1.0 - s))
            last[t] = (source[t].astype(F32) + v * s).astype(BF)
        logit = logit + dot_nt(times_of(d, last, q), head_rows(d, head, q, False))
    chance = jax.nn.sigmoid(logit)
    lane = lax.broadcasted_iota(jnp.int32, (d.rows, d.lanes), 1)
    live = alive_mask(d, tab[0]) & (lane < d.times)
    chance = jnp.where(live, chance, 0.0)
    write_prob(d, chance, plane, prob)
    g = jnp.where(live, chance - read_labels(d, labels, plane), 0.0)
    coarse = g.astype(BF).astype(F32)
    pair = (coarse + pltpu.roll(g - coarse, d.times, 1)).astype(BF)
    g_out[...] = pair
    grad_e = jnp.zeros((d.rank, d.channels), F32)
    grad_h = jnp.zeros((1, d.channels), F32)
    for q in range(d.tiles):
        up = dot(pair, head_rows(d, head, q, True))
        delta = jnp.concatenate(
            [
                up[:, j * d.channels : (j + 1) * d.channels] * slope[q * d.group + j]
                for j in range(d.group)
            ],
            axis=1,
        ).astype(BF)
        value = dot_nt(delta, expand).astype(BF)
        own_out[q] = value
        own[q] = value.astype(F32)
        grad_e = grad_e + diag_sum(d, dot_tn(mixed[q], delta))
        total = dot_tn(pair, times_of(d, last, q))
        for j in range(d.group):
            t = q * d.group + j
            at = slice(j * d.channels, (j + 1) * d.channels)
            grad_h = grad_h + total[t : t + 1, at] + total[d.times + t : d.times + t + 1, at]
    expand_grad[...] = grad_e
    head_grad[...] = jnp.concatenate([grad_h, jnp.zeros((SUB - 1, d.channels), F32)], axis=0)
    write_send(d, tab, own, send)
    save.wait()


def core_kernel(d, around_hbm, own, out, shifted, sems):
    copies = Copies(sems, [(around_hbm, shifted)])
    copies.wait(0)
    core_gradient(d, shifted, own, out)


def back_two_kernel(
    d, tab_in, own_in, recv, core_hbm, reduce_hbm, expand_hbm, head_hbm, source, mixed, g_in, around_hbm, core_two,
    expand_two, head_grad, own_out, send, wide, shifted, conv, own, flat, inner, outer, core, reduce_ref, expand_ref,
    head_ref, around, packed, tab, sems,
):
    copies = Copies(
        sems,
        [
            (tab_in, tab), (core_hbm, core), (reduce_hbm, reduce_ref), (expand_hbm, expand_ref),
            (head_hbm, head_ref), (around_hbm, around),
        ],
    )
    copies.wait(0)
    fill(d, tab, own_in, recv, wide, shifted)
    copies.wait(1, 2, 3, 4)
    bands(d, core, flat, inner, outer, True)
    convolve(d, shifted, inner, outer, -1, conv)
    expand = block_diag(d, expand_ref[...])
    weight = block_diag(d, permuted_rows(d, reduce_ref[...]))
    head = head_ref[...]
    alive = alive_mask(d, tab[0])
    pair = g_in[...]
    grad_r = jnp.zeros((d.rank, d.channels), F32)
    grad_e = jnp.zeros((d.rank, d.channels), F32)
    for q in range(d.tiles):
        da = jnp.where(alive, trimmed(d, conv[q]), 0.0).astype(BF)
        grad_r = grad_r + diag_sum(d, dot_tn(da, times_of(d, source, q)))
        up = dot(
            jnp.concatenate([da, pair], axis=1),
            jnp.concatenate([weight, head_rows(d, head, q, True)], axis=0),
        )
        b = mixed[q]
        y = dot(b, expand)
        parts = []
        for j in range(d.group):
            at = slice(j * d.channels, (j + 1) * d.channels)
            v = y[:, at]
            s = sigmoid(v)
            parts.append((up[:, at] * (s * (1.0 + v * (1.0 - s)))).astype(BF))
        delta = jnp.concatenate(parts, axis=1)
        value = dot_nt(delta, expand).astype(BF)
        own_out[q] = value
        own[q] = value.astype(F32)
        grad_e = grad_e + diag_sum(d, dot_tn(b, delta))
    copies.wait(5)
    off = d.offsets
    core_gradient(d, around, own_out, packed)
    packed[off[1] : off[2], :] = core_two[...]
    packed[off[2] : off[3], :] = grad_e
    packed[off[3] : off[4], :] = grad_r
    packed[off[4] : off[5], :] = expand_two[...]
    packed[off[5] : off[6], :] = head_grad[...]
    rest = d.nspace * d.share - off[6]
    if rest:
        packed[off[6] :, :] = jnp.zeros((rest, d.channels), F32)
    write_send(d, tab, own, send)

    def put(n, carry):
        at = pl.multiple_of(n * d.share, SUB)
        send[n, d.block :, :] = packed[pl.ds(at, d.share), :].astype(BF)
        return carry

    lax.fori_loop(0, d.nspace, put, 0)


def back_one_kernel(
    d, tab_in, own_in, recv, core_hbm, source, send, wide, shifted, conv, flat, inner, outer, core, tab, sems
):
    copies = Copies(sems, [(tab_in, tab), (core_hbm, core)])
    copies.wait(0)
    fill(d, tab, own_in, recv, wide, shifted)
    copies.wait(1)
    bands(d, core, flat, inner, outer, True)
    convolve(d, shifted, inner, outer, -1, conv)
    alive = alive_mask(d, tab[0])
    grad_r = jnp.zeros((d.rank, d.channels), F32)
    for q in range(d.tiles):
        da = jnp.where(alive, trimmed(d, conv[q]), 0.0).astype(BF)
        grad_r = grad_r + diag_sum(d, dot_tn(da, times_of(d, source, q)))

    def add(n, total):
        return total + recv[n, d.block :, :].astype(F32)

    shares = lax.fori_loop(0, d.nspace, add, jnp.zeros((d.share, d.channels), F32))
    out = jnp.concatenate([grad_r, shares], axis=0).astype(BF)

    def put(n, carry):
        send[n] = out
        return carry

    lax.fori_loop(0, d.nspace, put, 0)


def unpack_kernel(d, recv, reduce_one, core_one, expand_one, reduce_two, core_two, expand_two, head, packed):
    off = d.offsets
    high = d.rank // d.group
    scale = 1.0 / d.cells

    def take(n, total):
        at = pl.multiple_of(n * d.share, SUB)
        packed[pl.ds(at, d.share), :] = recv[n, d.rank :, :].astype(F32) * scale
        return total + recv[n, : d.rank, :].astype(F32)

    first = lax.fori_loop(0, d.nspace, take, jnp.zeros((d.rank, d.channels), F32)) * scale
    for at, core in ((off[0], core_one), (off[1], core_two)):
        for rh in range(high):
            core[:, rh * d.lanes : (rh + 1) * d.lanes] = packed[pl.ds(at + rh, 27, stride=high), :]
    second = packed[off[3] : off[4], :]
    for value, ref in ((first, reduce_one), (second, reduce_two)):
        for rl in range(d.group):
            ref[pl.ds(rl, high, stride=d.group), :] = value[rl * high : (rl + 1) * high]
    expand_one[...] = packed[off[2] : off[3], :]
    expand_two[...] = packed[off[4] : off[5], :]
    head[...] = packed[off[5] : off[5] + 1, :]


VM = pl.BlockSpec(memory_space=pltpu.VMEM)
SM = pl.BlockSpec(memory_space=pltpu.SMEM)
HB = pl.BlockSpec(memory_space=pltpu.HBM)


def call(kernel, d, name, ins, outs, scratch, operands, limit=LIMIT):
    shapes = tuple(jax.ShapeDtypeStruct(s, t) for s, t, _ in outs)
    specs = tuple(m for _, _, m in outs)
    return pl.pallas_call(
        functools.partial(kernel, d),
        out_shape=shapes,
        in_specs=list(ins),
        out_specs=specs,
        scratch_shapes=scratch,
        name=name,
        compiler_params=pltpu.CompilerParams(vmem_limit_bytes=limit),
    )(*operands)


def on_device(
    volume, labels, run_lengths, run_owner, reduce_one, core_one, expand_one, reduce_two, core_two, expand_two,
    head_vector,
):
    nspace = lax.axis_size("space")
    slots, edge, _, times, channels = volume.shape
    rank = reduce_one.shape[0]
    d = Dims(nspace, slots, edge, times, channels, rank, run_lengths.shape[0], run_lengths.shape[1])
    me = lax.axis_index("space").astype(jnp.int32).reshape(1)
    head = head_vector.reshape(1, channels)
    own_shape = (d.tiles, d.rows, d.lanes)
    wide_shape = (d.times, d.rows, d.channels)
    send_shape = (nspace, d.block, channels)
    shifted_shape = (3, d.span, d.tiles * d.lanes)
    size = 2 * d.lanes
    core_shape = (27 * rank // d.group, d.lanes)
    own_f = pltpu.VMEM(own_shape, F32)
    rim = pltpu.VMEM((d.tiles, d.span + 2 * SUB, d.lanes), F32)
    shifted = pltpu.VMEM(shifted_shape, BF)
    conv = pltpu.VMEM((d.tiles, d.core_rows, d.lanes), F32)
    flat = pltpu.VMEM(core_shape, F32)
    down = [pltpu.VMEM((9 * size, size), BF)] * 2
    across = [pltpu.VMEM((size, 9 * size), BF)] * 2
    core_v = pltpu.VMEM(core_one.shape, BF)
    factor = pltpu.VMEM((rank, channels), BF)
    tab_s = pltpu.SMEM((d.t_size,), jnp.int32)
    small = ((rank, channels), F32, VM)

    def sems(n):
        return pltpu.SemaphoreType.DMA((n,))

    def exchange(send):
        return lax.all_to_all(send, "space", split_axis=0, concat_axis=0, tiled=True)

    tab, xt, a1, send = call(
        first_kernel, d, "first", [SM, HB, HB, HB, HB],
        [((d.t_size,), jnp.int32, VM), (wide_shape, BF, VM), (own_shape, BF, VM), (send_shape, BF, VM)],
        [
            pltpu.VMEM((edge, slots, edge, times, channels), BF),
            pltpu.VMEM((d.rows * times, channels), F32),
            own_f, factor, pltpu.SMEM(run_lengths.shape, jnp.int32), pltpu.SMEM(run_owner.shape, jnp.int32), tab_s,
            sems(edge + 4),
        ],
        [me, run_lengths, run_owner, volume, reduce_one],
    )
    recv = exchange(send)
    b1, h1, a2, send, around1 = call(
        layer_one_kernel, d, "layer_one", [VM, VM, VM, HB, HB, HB, VM],
        [
            (own_shape, BF, VM), (wide_shape, BF, VM), (own_shape, BF, VM), (send_shape, BF, VM),
            (shifted_shape, BF, HB),
        ],
        [rim, shifted, conv, own_f, flat] + down + [core_v, factor, factor, tab_s, sems(5)],
        [tab, a1, recv, core_one, expand_one, reduce_two, xt],
    )
    recv = exchange(send)
    db2, send, prob, g, eg2, hg, around2 = call(
        layer_two_kernel, d, "layer_two", [VM, VM, VM, HB, HB, HB, VM, HB],
        [
            (own_shape, BF, VM), (send_shape, BF, VM), (labels.shape, F32, VM), ((d.rows, d.lanes), BF, VM),
            small, ((SUB, channels), F32, VM), (shifted_shape, BF, HB),
        ],
        [
            rim, shifted, conv, own_f, pltpu.VMEM(wide_shape, F32), pltpu.VMEM(wide_shape, BF),
            pltpu.VMEM(own_shape, BF), flat,
        ]
        + down
        + [core_v, factor, pltpu.VMEM((1, channels), BF), pltpu.VMEM(labels.shape, jnp.int32), pltpu.VMEM((d.width, d.lanes), F32), tab_s, sems(6)],
        [tab, a2, recv, core_two, expand_two, head, h1, labels],
    )
    recv = exchange(send)
    (cg2,) = call(
        core_kernel, d, "core_two", [HB, VM], [(core_shape, F32, VM)], [shifted, sems(1)], [around2, db2]
    )
    db1, send = call(
        back_two_kernel, d, "back_two", [VM, VM, VM, HB, HB, HB, HB, VM, VM, VM, HB, VM, VM, VM],
        [(own_shape, BF, VM), ((nspace, d.block + d.share, channels), BF, VM)],
        [rim, shifted, conv, own_f, flat]
        + across
        + [
            core_v, factor, factor, pltpu.VMEM((1, channels), BF), shifted,
            pltpu.VMEM((nspace * d.share, channels), F32), tab_s, sems(6),
        ],
        [tab, db2, recv, core_two, reduce_two, expand_one, head, h1, b1, g, around1, cg2, eg2, hg],
    )
    recv = exchange(send)
    (send,) = call(
        back_one_kernel, d, "back_one", [VM, VM, VM, HB, VM],
        [((nspace, rank + d.share, channels), BF, VM)],
        [rim, shifted, conv, flat] + across + [core_v, tab_s, sems(2)],
        [tab, db1, recv, core_one, xt],
    )
    recv = exchange(send)
    core_out = ((27, rank * rank), F32, VM)
    r1, c1, e1, r2, c2, e2, hv = call(
        unpack_kernel, d, "unpack", [VM],
        [small, core_out, small, small, core_out, small, ((1, channels), F32, VM)],
        [pltpu.VMEM((nspace * d.share, channels), F32)], [recv],
    )
    return prob, r1, c1, e1, r2, c2, e2, hv.reshape(channels)


def solution(mesh):
    in_specs = (
        P(("groups", "space"), None, None, None, None),
        P(("groups", "space"), None),
        P("groups", None),
        P("groups"),
    ) + (P(),) * 7
    out_specs = (P(("groups", "space"), None),) + (P("groups", None),) * 6 + (P("groups"),)
    return jax.shard_map(on_device, mesh=mesh, in_specs=in_specs, out_specs=out_specs, check_vma=False)
```

```python
import functools

import jax
import jax.numpy as jnp
from jax import lax
from jax.experimental import pallas as pl
from jax.experimental.pallas import tpu as pltpu
from jax.sharding import PartitionSpec as P

BF = jnp.bfloat16
F32 = jnp.float32
SUB = 8
LIMIT = 24 * 1024 * 1024


class Dims:
    def __init__(self, nspace, slots, edge, times, channels, rank, pairs, row_runs):
        self.nspace, self.slots, self.edge, self.times = nspace, slots, edge, times
        self.channels, self.rank, self.pairs, self.row_runs = channels, rank, pairs, row_runs
        self.lanes = channels
        self.group = channels // rank
        self.tiles = times // self.group
        self.width = slots * edge
        self.rows = edge * self.width
        self.line = self.width + SUB
        self.lines = edge + 2
        self.span = self.lines * self.line
        self.cells = edge * edge * times
        self.taps = 9
        self.t_send = 5
        self.t_recv = self.t_send + 2 * (1 + row_runs)
        self.t_size = self.t_recv + 2 * 3 * (slots + 2)
        self.part = self.tiles * SUB
        self.block = slots * self.part
        per_row = rank * rank // channels
        sizes = [27 * per_row, 27 * per_row, rank, rank, rank, SUB]
        self.offsets = [sum(sizes[:i]) for i in range(len(sizes) + 1)]
        self.share = -(-self.offsets[-1] // (nspace * SUB)) * SUB


def dot(a, b):
    return lax.dot_general(a, b, (((1,), (0,)), ((), ())), preferred_element_type=F32)


def dot_nt(a, b):
    return lax.dot_general(a, b, (((1,), (1,)), ((), ())), preferred_element_type=F32)


def dot_tn(a, b):
    return lax.dot_general(a, b, (((0,), (0,)), ((), ())), preferred_element_type=F32)


def halved(w):
    return (w.astype(F32) * 0.5).astype(BF)


def silu(u):
    return u + u * jnp.tanh(u)


def slope_twice(u, th):
    return (1.0 + th) * (1.0 + u * (1.0 - th))


def block_diag(d, w):
    rows = []
    for j in range(d.group):
        parts = [w if i == j else jnp.zeros_like(w) for i in range(d.group)]
        rows.append(jnp.concatenate(parts, axis=1))
    return jnp.concatenate(rows, axis=0)


def permuted_rows(d, w):
    high = d.rank // d.group
    to = lax.broadcasted_iota(jnp.int32, (d.rank, d.rank), 0)
    at = lax.broadcasted_iota(jnp.int32, (d.rank, d.rank), 1)
    pick = (at == (to % high) * d.group + to // high).astype(F32).astype(BF)
    return dot(pick, w).astype(BF)


def head_rows(d, head, q, twice):
    row = lax.broadcasted_iota(jnp.int32, (d.lanes, d.channels), 0)
    wide = jnp.broadcast_to(head.astype(F32), (d.lanes, d.channels))
    parts = []
    for j in range(d.group):
        t = q * d.group + j
        hit = row == t
        if twice:
            hit = hit | (row == d.times + t)
        parts.append(jnp.where(hit, wide, 0.0))
    return jnp.concatenate(parts, axis=1).astype(BF)


def alive_mask(d, length):
    i = lax.broadcasted_iota(jnp.int32, (d.edge, d.width, d.lanes), 1)
    return (i < length * d.edge).reshape(d.rows, d.lanes)


def times_of(d, ref, q):
    return jnp.concatenate([ref[q * d.group + j] for j in range(d.group)], axis=1)


def diag_sum(d, total):
    out = None
    for j in range(d.group):
        part = total[j * d.rank : (j + 1) * d.rank, j * d.channels : (j + 1) * d.channels]
        out = part if out is None else out + part
    return out


def make_table(d, me, lengths, owner, tab):
    my_run = lax.fori_loop(0, d.nspace, lambda k, s: s + jnp.where(owner[k] == me, k, 0), jnp.int32(0))
    row = my_run // d.row_runs
    place = my_run % d.row_runs
    pair = row // 2
    start = jnp.int32(0)
    total = jnp.int32(0)
    for r in range(d.row_runs):
        one = lengths[pair, r]
        start = start + jnp.where(place > r, one, 0)
        total = total + one
    length = lengths[pair, place]
    row_count = d.nspace // d.row_runs
    tab[0] = length
    tab[1] = (place > 0).astype(jnp.int32)
    tab[2] = owner[jnp.maximum(my_run - 1, 0)]
    tab[3] = (place < d.row_runs - 1).astype(jnp.int32)
    tab[4] = owner[jnp.minimum(my_run + 1, d.nspace - 1)]
    for side, step in ((0, -1), (1, 1)):
        target = row + step
        valid = (target >= 0) & (target < row_count)
        there = jnp.clip(target, 0, row_count - 1)
        base = d.t_send + side * (1 + d.row_runs)
        tab[base] = valid.astype(jnp.int32)
        for r in range(d.row_runs):
            tab[base + 1 + r] = owner[there * d.row_runs + r]
        starts = []
        at = jnp.int32(0)
        for r in range(d.row_runs):
            starts.append(at)
            at = at + lengths[there // 2, r]
        for n in range(d.slots + 2):
            s = n - 1
            p = start + s
            ok = valid & (p >= 0) & (p < total) & (s <= length)
            run, first = jnp.int32(0), jnp.int32(0)
            for r in range(1, d.row_runs):
                past = starts[r] <= p
                run = jnp.where(past, r, run)
                first = jnp.where(past, starts[r], first)
            base = d.t_recv + (side * (d.slots + 2) + n) * 3
            tab[base] = ok.astype(jnp.int32)
            tab[base + 1] = owner[there * d.row_runs + run]
            tab[base + 2] = jnp.where(ok, p - first, 0)


def write_send(d, tab, own, send):
    for side, line in ((0, 0), (1, d.edge - 1)):
        base = d.t_send + side * (1 + d.row_runs)
        blocks = []
        for s in range(d.slots):
            at = line * d.width + s * d.edge
            blocks.append(
                jnp.concatenate([own[q, at : at + d.edge, :] for q in range(d.tiles)], axis=0).astype(BF)
            )

        @pl.when(tab[base] == 1)
        def _(base=base, blocks=blocks):
            for r in range(d.row_runs):
                for s in range(d.slots):
                    send[tab[base + 1 + r], s * d.part : (s + 1) * d.part, :] = blocks[s]

    length = tab[0]
    for flag, to, at in ((1, 2, 0), (3, 4, length * d.edge - 1)):
        end = jnp.concatenate(
            [own[q, pl.ds(at, d.edge, stride=d.width), :] for q in range(d.tiles)], axis=0
        ).astype(BF)

        @pl.when(tab[flag] == 1)
        def _(to=to, end=end):
            send[tab[to], : d.part, :] = end


def fill(d, tab, own, recv, wide, even, odd):
    length = tab[0]
    for q in range(d.tiles):
        zero = jnp.zeros((SUB, d.lanes), F32)
        wide[q, :SUB, :] = zero
        for n in range(d.lines):
            at = SUB + d.line * n + d.width
            wide[q, at : at + SUB, :] = zero
        value = own[q].astype(F32)
        for c in range(d.edge):
            at = SUB + d.line * (c + 1)
            wide[q, at : at + d.width, :] = value[c * d.width : (c + 1) * d.width]
    first = SUB + d.line
    for flag, source, at in ((1, 2, first - 1), (3, 4, first + length * d.edge)):
        keep = tab[flag] == 1
        end = recv[tab[source], : d.part, :].astype(F32)
        end = jnp.where(keep, end, 0.0)
        for q in range(d.tiles):
            wide[q, pl.ds(at, d.edge, stride=d.line), :] = end[q * SUB : (q + 1) * SUB]
    sub = lax.broadcasted_iota(jnp.int32, (SUB, d.lanes), 0)
    for side, line in ((0, 0), (1, d.lines - 1)):
        at = SUB + d.line * line
        for n in range(d.slots + 2):
            s = n - 1
            base = d.t_recv + (side * (d.slots + 2) + n) * 3
            keep = tab[base] == 1
            value = recv[tab[base + 1], pl.ds(pl.multiple_of(tab[base + 2] * d.part, d.part), d.part), :]
            value = jnp.where(keep, value.astype(F32), 0.0)
            for q in range(d.tiles):
                part = value[q * SUB : (q + 1) * SUB]
                if s < 0:
                    wide[q, at - 1 : at, :] = part[SUB - 1 : SUB]
                elif s == d.slots:
                    wide[q, at + s * SUB : at + s * SUB + 1, :] = part[0:1]
                else:
                    wide[q, at + s * SUB : (at + s * SUB) + SUB, :] = jnp.where((sub == 0) | (s < length), part, 0.0)
    for di in (-1, 0, 1):
        for q in range(d.tiles):
            lines = [
                wide[q, SUB + d.line * n + di : SUB + d.line * n + di + d.width, :] for n in range(d.lines)
            ]
            at = slice(q * d.lanes, (q + 1) * d.lanes)
            even[di + 1, :, at] = jnp.concatenate(lines, axis=0).astype(BF)
            odd[di + 1, :, at] = jnp.concatenate(lines[1:-1], axis=0).astype(BF)


def windows(d, views, direction, first, count):
    even, odd = views
    parts = []
    for di in (-1, 0, 1):
        for dc in (-1, 0, 1):
            col = slice(first * d.lanes, (first + count) * d.lanes)
            n = 1 + direction * di
            if dc == 0:
                parts.append(odd[n, :, col])
            else:
                at = d.width * (1 + direction * dc)
                parts.append(even[n, at : at + d.rows, col])
    return parts


def bands(d, core, flat, inner, outer, inner_t, outer_t):
    rank, group, lanes = d.rank, d.group, d.lanes
    high = rank // group
    for rh in range(high):
        flat[pl.ds(rh, 27, stride=high), :] = core[:, rh * lanes : (rh + 1) * lanes].astype(F32)
    rows = flat[...].astype(BF)
    at = lax.broadcasted_iota(jnp.int32, (lanes, lanes), 0)
    to = lax.broadcasted_iota(jnp.int32, (lanes, lanes), 1)
    spread = []
    for rl in range(group):
        pick = (at == rl * rank + to % rank).astype(F32).astype(BF)
        spread.append(dot(rows, pick))
    lane = lax.broadcasted_iota(jnp.int32, (rank, lanes), 1) // rank
    zero = jnp.zeros((rank, lanes), BF)
    size = 2 * lanes
    for k in range(d.taps):
        full = []
        for dt in (-1, 0, 1):
            o = 3 * k + dt + 1
            full.append(
                jnp.concatenate([spread[rl][o * high : (o + 1) * high] for rl in range(group)], axis=0)
            )
        cache = {}
        for delta in range(-1, group + 1):
            value = jnp.zeros((rank, lanes), F32)
            for dt in (-1, 0, 1):
                value = jnp.where(lane == delta - dt, full[dt + 1], value)
            cache[delta] = value.astype(BF)
        for down in range(2 * group):
            row = slice(down * rank, (down + 1) * rank)
            for across in range(2):
                value = cache.get(down - across * group, zero)
                inner[k * size + down * rank : k * size + (down + 1) * rank, across * lanes : (across + 1) * lanes] = value
                inner_t[row, k * size + across * lanes : k * size + (across + 1) * lanes] = value
            far = cache[-1] if down == group - 1 else cache[group] if down == group else zero
            outer_t[row, k * lanes : (k + 1) * lanes] = far
        for down in range(group):
            row = slice(k * lanes + down * rank, k * lanes + (down + 1) * rank)
            outer[row, :lanes] = cache[group] if down == 0 else zero
            outer[row, lanes:] = cache[-1] if down == group - 1 else zero


def convolve(d, views, inner, outer, direction, out):
    mul = dot if direction == 1 else dot_nt
    half = d.tiles // 2
    stacked = [
        jnp.concatenate(windows(d, views, direction, 2 * p, 2), axis=1) for p in range(half)
    ]
    total = mul(jnp.concatenate(stacked, axis=0), inner[...])
    for p in range(half):
        for n in range(2):
            out[2 * p + n] = total[p * d.rows : (p + 1) * d.rows, n * d.lanes : (n + 1) * d.lanes]
    lane = lax.broadcasted_iota(jnp.int32, (d.rows, d.lanes), 1) // d.rank
    for p in range(half - 1):
        before = windows(d, views, direction, 2 * p + 1, 1)
        after = windows(d, views, direction, 2 * p + 2, 1)
        mixed = [jnp.where(lane == d.group - 1, x, y) for x, y in zip(before, after)]
        total = mul(jnp.concatenate(mixed, axis=1), outer[...])
        for n in range(2):
            q = 2 * p + 1 + n
            out[q] = out[q] + total[:, n * d.lanes : (n + 1) * d.lanes]


def core_gradient(d, views, own, out):
    lane = lax.broadcasted_iota(jnp.int32, (1, d.lanes), 1) // d.rank
    tiles = [own[q].astype(F32) for q in range(d.tiles)]
    right = []
    zero = jnp.zeros_like(tiles[0])
    for q in range(d.tiles):
        after = tiles[q + 1] if q + 1 < d.tiles else zero
        before = tiles[q - 1] if q > 0 else zero
        mixed = jnp.where(lane == 0, after, jnp.where(lane == d.group - 1, before, 0.0))
        right.append(jnp.concatenate([tiles[q], mixed], axis=1).astype(BF))
    right = jnp.concatenate(right, axis=0)
    rank, group = d.rank, d.group
    high = rank // group
    wide_lane = lax.broadcasted_iota(jnp.int32, (high, d.lanes), 1) // rank
    for k in range(d.taps):
        left = jnp.concatenate([windows(d, views, 1, q, 1)[k] for q in range(d.tiles)], axis=0)
        total = dot_tn(left, right)
        for dt in (-1, 0, 1):
            pieces = []
            for j in range(group):
                if 0 <= j + dt < group:
                    row, col = j + dt, 0
                elif j + dt == group:
                    row, col = 0, 1
                else:
                    row, col = group - 1, 1
                pieces.append(total[row * rank : (row + 1) * rank, col * d.lanes : (col + 1) * d.lanes])
            result = None
            for turn in range(group):
                mix = None
                for j in range(group):
                    rl = (j + turn) % group
                    part = pieces[j][rl * high : (rl + 1) * high]
                    mix = part if mix is None else jnp.where(wide_lane == j, part, mix)
                if turn:
                    mix = pltpu.roll(mix, turn * rank, 1)
                result = mix if result is None else result + mix
            o = 3 * k + dt + 1
            out[o * high : (o + 1) * high, :] = result


class Copies:
    def __init__(self, sems, pairs):
        self.all = [pltpu.make_async_copy(a, b, sems.at[n]) for n, (a, b) in enumerate(pairs)]
        for one in self.all:
            one.start()

    def wait(self, *which):
        for n in which:
            self.all[n].wait()


def start_kernel(d, me, token):
    token[...] = jnp.zeros((SUB, d.lanes), F32) + me[0].astype(F32)


def first_kernel(
    d, me, lengths_hbm, owner_hbm, x_hbm, reduce_hbm, core_one_hbm, core_two_hbm, token, *refs
):
    del token
    tab_out, xt, own_out, send = refs[:4]
    band_refs = refs[4:12]
    xc, xf, own, lengths, owner, reduce_ref, core_one, core_two, flat, tab, sems = refs[12:]
    copies = Copies(
        sems,
        [
            (lengths_hbm, lengths), (owner_hbm, owner), (reduce_hbm, reduce_ref), (core_one_hbm, core_one),
            (core_two_hbm, core_two),
        ]
        + [(x_hbm.at[:, :, c], xc.at[c]) for c in range(d.edge)],
    )
    copies.wait(0, 1, 2, 3, 4)
    make_table(d, me[0], lengths, owner, tab)
    weight = block_diag(d, permuted_rows(d, reduce_ref[...]))
    bands(d, core_one, flat, *band_refs[0:4])
    bands(d, core_two, flat, *band_refs[4:8])
    save = pltpu.make_async_copy(tab, tab_out, sems.at[d.edge + 5])
    save.start()
    per_line = d.width * d.times
    for c in range(d.edge):
        copies.wait(5 + c)
        xf[c * per_line : (c + 1) * per_line, :] = xc[c].reshape(per_line, d.channels).astype(F32)
    alive = alive_mask(d, tab[0])
    for q in range(d.tiles):
        for j in range(d.group):
            t = q * d.group + j
            xt[t] = xf[pl.ds(t, d.rows, stride=d.times), :].astype(BF)
        value = dot_nt(times_of(d, xt, q), weight)
        value = jnp.where(alive, value, 0.0).astype(BF)
        own_out[q] = value
        own[q] = value.astype(F32)
    write_send(d, tab, own, send)
    save.wait()


def layer_one_kernel(
    d, tab_in, own_in, recv, inner, outer, expand_ref, reduce_next, source, mixed, hidden, own_out, send, even, odd,
    wide, conv, own, tab, sems,
):
    Copies(sems, [(tab_in, tab)]).wait(0)
    fill(d, tab, own_in, recv, wide, even, odd)
    convolve(d, (even, odd), inner, outer, 1, conv)
    expand = block_diag(d, expand_ref[...])
    half = halved(expand)
    weight = block_diag(d, permuted_rows(d, reduce_next[...]))
    alive = alive_mask(d, tab[0])
    for q in range(d.tiles):
        b = conv[q].astype(BF)
        mixed[q] = b
        y = dot(b, half)
        for j in range(d.group):
            t = q * d.group + j
            u = y[:, j * d.channels : (j + 1) * d.channels]
            hidden[t] = (source[t].astype(F32) + silu(u)).astype(BF)
        value = dot_nt(times_of(d, hidden, q), weight)
        value = jnp.where(alive, value, 0.0).astype(BF)
        own_out[q] = value
        own[q] = value.astype(F32)
    write_send(d, tab, own, send)


def read_labels(d, labels, plane):
    for i in range(d.edge):
        part = labels[:, i * d.lanes : (i + 1) * d.lanes].astype(F32)
        plane[pl.ds(i, d.slots, stride=d.edge), :] = part
    value = plane[...]
    lines = [value if c == 0 else pltpu.roll(value, d.lanes - c * d.times, 1) for c in range(d.edge)]
    return jnp.concatenate(lines, axis=0)


def write_prob(d, chance, plane, prob):
    total = chance[: d.width]
    for c in range(1, d.edge):
        total = total + pltpu.roll(chance[c * d.width : (c + 1) * d.width], c * d.times, 1)
    plane[...] = total
    for i in range(d.edge):
        prob[:, i * d.lanes : (i + 1) * d.lanes] = plane[pl.ds(i, d.slots, stride=d.edge), :]


def layer_two_kernel(
    d, tab_in, own_in, recv, inner, outer, expand_ref, head_ref, source, labels, own_out, send, prob, g_out,
    expand_grad, head_grad, core_grad, wide, even, odd, conv, own, slope, last, mixed, plane, tab, sems,
):
    Copies(sems, [(tab_in, tab)]).wait(0)
    fill(d, tab, own_in, recv, wide, even, odd)
    convolve(d, (even, odd), inner, outer, 1, conv)
    expand = block_diag(d, expand_ref[...])
    half = halved(expand)
    head = head_ref[...]
    logit = jnp.zeros((d.rows, d.lanes), F32)
    for q in range(d.tiles):
        b = conv[q].astype(BF)
        mixed[q] = b
        y = dot(b, half)
        for j in range(d.group):
            t = q * d.group + j
            u = y[:, j * d.channels : (j + 1) * d.channels]
            th = jnp.tanh(u)
            slope[t] = slope_twice(u, th)
            last[t] = (source[t].astype(F32) + (u + u * th)).astype(BF)
        logit = logit + dot_nt(times_of(d, last, q), head_rows(d, head, q, False))
    chance = jax.nn.sigmoid(logit)
    lane = lax.broadcasted_iota(jnp.int32, (d.rows, d.lanes), 1)
    live = alive_mask(d, tab[0]) & (lane < d.times)
    chance = jnp.where(live, chance, 0.0)
    write_prob(d, chance, plane, prob)
    g = jnp.where(live, chance - read_labels(d, labels, plane), 0.0)
    coarse = g.astype(BF).astype(F32)
    pair = (coarse + pltpu.roll(g - coarse, d.times, 1)).astype(BF)
    g_out[...] = pair
    grad_e = jnp.zeros((d.rank, d.channels), F32)
    grad_h = jnp.zeros((1, d.channels), F32)
    for q in range(d.tiles):
        up = dot(pair, halved(head_rows(d, head, q, True)))
        delta = jnp.concatenate(
            [
                up[:, j * d.channels : (j + 1) * d.channels] * slope[q * d.group + j]
                for j in range(d.group)
            ],
            axis=1,
        ).astype(BF)
        value = dot_nt(delta, expand).astype(BF)
        own_out[q] = value
        own[q] = value.astype(F32)
        grad_e = grad_e + diag_sum(d, dot_tn(mixed[q], delta))
        total = dot_tn(pair, times_of(d, last, q))
        for j in range(d.group):
            t = q * d.group + j
            at = slice(j * d.channels, (j + 1) * d.channels)
            grad_h = grad_h + total[t : t + 1, at] + total[d.times + t : d.times + t + 1, at]
    expand_grad[...] = grad_e
    head_grad[...] = jnp.concatenate([grad_h, jnp.zeros((SUB - 1, d.channels), F32)], axis=0)
    core_gradient(d, (even, odd), own_out, core_grad)
    write_send(d, tab, own, send)


def back_two_kernel(
    d, tab_in, own_in, recv, inner, outer, reduce_ref, expand_ref, head_ref, source, mixed, g_in, first_even, first_odd,
    core_two, expand_two, head_grad, own_out, send, wide, even, odd, conv, own, packed, tab, sems,
):
    Copies(sems, [(tab_in, tab)]).wait(0)
    fill(d, tab, own_in, recv, wide, even, odd)
    convolve(d, (even, odd), inner, outer, -1, conv)
    expand = block_diag(d, expand_ref[...])
    half = halved(expand)
    weight = block_diag(d, permuted_rows(d, reduce_ref[...]))
    head = head_ref[...]
    alive = alive_mask(d, tab[0])
    pair = g_in[...]
    grad_r = jnp.zeros((d.rank, d.channels), F32)
    grad_e = jnp.zeros((d.rank, d.channels), F32)
    for q in range(d.tiles):
        da = jnp.where(alive, conv[q], 0.0).astype(BF)
        grad_r = grad_r + diag_sum(d, dot_tn(da, times_of(d, source, q)))
        up = dot(
            jnp.concatenate([da, pair], axis=1),
            halved(jnp.concatenate([weight, head_rows(d, head, q, True)], axis=0)),
        )
        b = mixed[q]
        y = dot(b, half)
        parts = []
        for j in range(d.group):
            at = slice(j * d.channels, (j + 1) * d.channels)
            u = y[:, at]
            parts.append((up[:, at] * slope_twice(u, jnp.tanh(u))).astype(BF))
        delta = jnp.concatenate(parts, axis=1)
        value = dot_nt(delta, expand).astype(BF)
        own_out[q] = value
        own[q] = value.astype(F32)
        grad_e = grad_e + diag_sum(d, dot_tn(b, delta))
    off = d.offsets
    core_gradient(d, (first_even, first_odd), own_out, packed)
    packed[off[1] : off[2], :] = core_two[...]
    packed[off[2] : off[3], :] = grad_e
    packed[off[3] : off[4], :] = grad_r
    packed[off[4] : off[5], :] = expand_two[...]
    packed[off[5] : off[6], :] = head_grad[...]
    rest = d.nspace * d.share - off[6]
    if rest:
        packed[off[6] :, :] = jnp.zeros((rest, d.channels), F32)
    write_send(d, tab, own, send)

    def put(n, carry):
        at = pl.multiple_of(n * d.share, SUB)
        send[n, d.block :, :] = packed[pl.ds(at, d.share), :].astype(BF)
        return carry

    lax.fori_loop(0, d.nspace, put, 0)


def back_one_kernel(d, tab_in, own_in, recv, inner, outer, source, send, wide, even, odd, conv, tab, sems):
    Copies(sems, [(tab_in, tab)]).wait(0)
    fill(d, tab, own_in, recv, wide, even, odd)
    convolve(d, (even, odd), inner, outer, -1, conv)
    alive = alive_mask(d, tab[0])
    grad_r = jnp.zeros((d.rank, d.channels), F32)
    for q in range(d.tiles):
        da = jnp.where(alive, conv[q], 0.0).astype(BF)
        grad_r = grad_r + diag_sum(d, dot_tn(da, times_of(d, source, q)))

    def add(n, total):
        return total + recv[n, d.block :, :].astype(F32)

    shares = lax.fori_loop(0, d.nspace, add, jnp.zeros((d.share, d.channels), F32))
    out = jnp.concatenate([grad_r, shares], axis=0).astype(BF)

    def put(n, carry):
        send[n] = out
        return carry

    lax.fori_loop(0, d.nspace, put, 0)


def unpack_kernel(d, recv, reduce_one, core_one, expand_one, reduce_two, core_two, expand_two, head, packed):
    off = d.offsets
    high = d.rank // d.group
    scale = 1.0 / d.cells

    def take(n, total):
        at = pl.multiple_of(n * d.share, SUB)
        packed[pl.ds(at, d.share), :] = recv[n, d.rank :, :].astype(F32) * scale
        return total + recv[n, : d.rank, :].astype(F32)

    first = lax.fori_loop(0, d.nspace, take, jnp.zeros((d.rank, d.channels), F32)) * scale
    for at, core in ((off[0], core_one), (off[1], core_two)):
        for rh in range(high):
            core[:, rh * d.lanes : (rh + 1) * d.lanes] = packed[pl.ds(at + rh, 27, stride=high), :]
    second = packed[off[3] : off[4], :]
    for value, ref in ((first, reduce_one), (second, reduce_two)):
        for rl in range(d.group):
            ref[pl.ds(rl, high, stride=d.group), :] = value[rl * high : (rl + 1) * high]
    expand_one[...] = packed[off[2] : off[3], :]
    expand_two[...] = packed[off[4] : off[5], :]
    head[...] = packed[off[5] : off[5] + 1, :]


VM = pl.BlockSpec(memory_space=pltpu.VMEM)
SM = pl.BlockSpec(memory_space=pltpu.SMEM)
HB = pl.BlockSpec(memory_space=pltpu.HBM)


def call(kernel, d, name, ins, outs, scratch, operands, cost=None):
    shapes = tuple(jax.ShapeDtypeStruct(s, t) for s, t, _ in outs)
    specs = tuple(m for _, _, m in outs)
    return pl.pallas_call(
        functools.partial(kernel, d),
        out_shape=shapes,
        in_specs=list(ins),
        out_specs=specs,
        scratch_shapes=scratch,
        name=name,
        cost_estimate=cost,
        compiler_params=pltpu.CompilerParams(vmem_limit_bytes=LIMIT),
    )(*operands)


def on_device(
    volume, labels, run_lengths, run_owner, reduce_one, core_one, expand_one, reduce_two, core_two, expand_two,
    head_vector,
):
    nspace = lax.axis_size("space")
    slots, edge, _, times, channels = volume.shape
    rank = reduce_one.shape[0]
    d = Dims(nspace, slots, edge, times, channels, rank, run_lengths.shape[0], run_lengths.shape[1])
    me = lax.axis_index("space").astype(jnp.int32).reshape(1)
    head = head_vector.reshape(1, channels)
    own_shape = (d.tiles, d.rows, d.lanes)
    wide_shape = (d.times, d.rows, d.channels)
    send_shape = (nspace, d.block, channels)
    even_shape = (3, d.lines * d.width, d.tiles * d.lanes)
    odd_shape = (3, d.rows, d.tiles * d.lanes)
    size = 2 * d.lanes
    core_shape = (27 * rank // d.group, d.lanes)
    own_f = pltpu.VMEM(own_shape, F32)
    rim = pltpu.VMEM((d.tiles, d.span + 2 * SUB, d.lanes), F32)
    views = [pltpu.VMEM(even_shape, BF), pltpu.VMEM(odd_shape, BF)]
    tab_s = pltpu.SMEM((d.t_size,), jnp.int32)
    small = ((rank, channels), F32, VM)
    own_o, wide_o, send_o = (own_shape, BF, VM), (wide_shape, BF, VM), (send_shape, BF, VM)
    band_shapes = [(9 * size, size), (9 * d.lanes, size), (size, 9 * size), (size, 9 * d.lanes)] * 2

    def sems(n):
        return pltpu.SemaphoreType.DMA((n,))

    def exchange(send):
        return lax.all_to_all(send, "space", split_axis=0, concat_axis=0, tiled=True)

    (token,) = call(
        start_kernel, d, "start", [SM], [((SUB, d.lanes), F32, VM)], [], [me],
        cost=pl.CostEstimate(flops=10**10, bytes_accessed=0, transcendentals=0),
    )
    tab, xt, a1, send, inner1, outer1, inner1t, outer1t, inner2, outer2, inner2t, outer2t = call(
        first_kernel, d, "first", [SM] + [HB] * 6 + [VM],
        [((d.t_size,), jnp.int32, VM), wide_o, own_o, send_o] + [(b, BF, VM) for b in band_shapes],
        [
            pltpu.VMEM((edge, slots, edge, times, channels), BF),
            pltpu.VMEM((d.rows * times, channels), F32),
            own_f, pltpu.SMEM(run_lengths.shape, jnp.int32), pltpu.SMEM(run_owner.shape, jnp.int32),
            pltpu.VMEM((rank, channels), BF), pltpu.VMEM(core_one.shape, BF), pltpu.VMEM(core_one.shape, BF),
            pltpu.VMEM(core_shape, F32), tab_s, sems(edge + 6),
        ],
        [me, run_lengths, run_owner, volume, reduce_one, core_one, core_two, token],
    )
    recv = exchange(send)
    b1, h1, a2, send, even1, odd1 = call(
        layer_one_kernel, d, "layer_one", [VM] * 8,
        [own_o, wide_o, own_o, send_o, (even_shape, BF, VM), (odd_shape, BF, VM)],
        [rim, own_f, own_f, tab_s, sems(1)],
        [tab, a1, recv, inner1, outer1, expand_one, reduce_two, xt],
    )
    recv = exchange(send)
    db2, send, prob, g, eg2, hg, cg2 = call(
        layer_two_kernel, d, "layer_two", [VM] * 9,
        [
            own_o, send_o, (labels.shape, F32, VM), ((d.rows, d.lanes), BF, VM), small, ((SUB, channels), F32, VM),
            (core_shape, F32, VM),
        ],
        [rim]
        + views
        + [
            own_f, own_f, pltpu.VMEM(wide_shape, F32), pltpu.VMEM(wide_shape, BF), pltpu.VMEM(own_shape, BF),
            pltpu.VMEM((d.width, d.lanes), F32), tab_s, sems(1),
        ],
        [tab, a2, recv, inner2, outer2, expand_two, head, h1, labels],
    )
    recv = exchange(send)
    db1, send = call(
        back_two_kernel, d, "back_two", [VM] * 16,
        [own_o, ((nspace, d.block + d.share, channels), BF, VM)],
        [rim] + views + [own_f, own_f, pltpu.VMEM((nspace * d.share, channels), F32), tab_s, sems(1)],
        [tab, db2, recv, inner2t, outer2t, reduce_two, expand_one, head, h1, b1, g, even1, odd1, cg2, eg2, hg],
    )
    recv = exchange(send)
    (send,) = call(
        back_one_kernel, d, "back_one", [VM] * 6,
        [((nspace, rank + d.share, channels), BF, VM)],
        [rim] + views + [own_f, tab_s, sems(1)],
        [tab, db1, recv, inner1t, outer1t, xt],
    )
    recv = exchange(send)
    core_out = ((27, rank * rank), F32, VM)
    r1, c1, e1, r2, c2, e2, hv = call(
        unpack_kernel, d, "unpack", [VM],
        [small, core_out, small, small, core_out, small, ((1, channels), F32, VM)],
        [pltpu.VMEM((nspace * d.share, channels), F32)], [recv],
    )
    return prob, r1, c1, e1, r2, c2, e2, hv.reshape(channels)


def solution(mesh):
    in_specs = (
        P(("groups", "space"), None, None, None, None),
        P(("groups", "space"), None),
        P("groups", None),
        P("groups"),
    ) + (P(),) * 7
    out_specs = (P(("groups", "space"), None),) + (P("groups", None),) * 6 + (P("groups"),)
    return jax.shard_map(on_device, mesh=mesh, in_specs=in_specs, out_specs=out_specs, check_vma=False)
```

```python
import functools

import jax
import jax.numpy as jnp
from jax import lax
from jax.experimental import pallas as pl
from jax.experimental.pallas import tpu as pltpu
from jax.sharding import PartitionSpec as P

BF = jnp.bfloat16
F32 = jnp.float32
SUB = 8
LIMIT = 24 * 1024 * 1024


class Dims:
    def __init__(self, nspace, slots, edge, times, channels, rank, pairs, row_runs):
        self.nspace, self.slots, self.edge, self.times = nspace, slots, edge, times
        self.channels, self.rank, self.pairs, self.row_runs = channels, rank, pairs, row_runs
        self.lanes = channels
        self.group = channels // rank
        self.tiles = times // self.group
        self.width = slots * edge
        self.rows = edge * self.width
        self.line = self.width + SUB
        self.lines = edge + 2
        self.span = self.lines * self.line
        self.cells = edge * edge * times
        self.taps = 9
        self.t_send = 5
        self.t_recv = self.t_send + 2 * (1 + row_runs)
        self.t_size = self.t_recv + 2 * 3 * (slots + 2)
        self.part = self.tiles * SUB
        self.block = slots * self.part
        core = 27 * rank * rank // channels
        self.two = [0, core, core + rank, core + rank + SUB]
        self.one = [0, core, core + rank, core + 2 * rank]
        self.share_two = -(-self.two[-1] // (nspace * SUB)) * SUB
        self.share_one = -(-self.one[-1] // (nspace * SUB)) * SUB


def dot(a, b):
    return lax.dot_general(a, b, (((1,), (0,)), ((), ())), preferred_element_type=F32)


def dot_nt(a, b):
    return lax.dot_general(a, b, (((1,), (1,)), ((), ())), preferred_element_type=F32)


def dot_tn(a, b):
    return lax.dot_general(a, b, (((0,), (0,)), ((), ())), preferred_element_type=F32)


def halved(w):
    return (w.astype(F32) * 0.5).astype(BF)


def silu(u):
    return u + u * jnp.tanh(u)


def slope_twice(u, th):
    return (1.0 + th) * (1.0 + u * (1.0 - th))


def block_diag(d, w):
    rows = []
    for j in range(d.group):
        parts = [w if i == j else jnp.zeros_like(w) for i in range(d.group)]
        rows.append(jnp.concatenate(parts, axis=1))
    return jnp.concatenate(rows, axis=0)


def permuted_rows(d, w):
    high = d.rank // d.group
    to = lax.broadcasted_iota(jnp.int32, (d.rank, d.rank), 0)
    at = lax.broadcasted_iota(jnp.int32, (d.rank, d.rank), 1)
    pick = (at == (to % high) * d.group + to // high).astype(F32).astype(BF)
    return dot(pick, w).astype(BF)


def head_rows(d, head, q, twice):
    row = lax.broadcasted_iota(jnp.int32, (d.lanes, d.channels), 0)
    wide = jnp.broadcast_to(head.astype(F32), (d.lanes, d.channels))
    parts = []
    for j in range(d.group):
        t = q * d.group + j
        hit = row == t
        if twice:
            hit = hit | (row == d.times + t)
        parts.append(jnp.where(hit, wide, 0.0))
    return jnp.concatenate(parts, axis=1).astype(BF)


def alive_mask(d, length):
    i = lax.broadcasted_iota(jnp.int32, (d.edge, d.width, d.lanes), 1)
    return (i < length * d.edge).reshape(d.rows, d.lanes)


def times_of(d, ref, q):
    return jnp.concatenate([ref[q * d.group + j] for j in range(d.group)], axis=1)


def diag_sum(d, total):
    out = None
    for j in range(d.group):
        part = total[j * d.rank : (j + 1) * d.rank, j * d.channels : (j + 1) * d.channels]
        out = part if out is None else out + part
    return out


def make_table(d, me, lengths, owner, tab):
    my_run = lax.fori_loop(0, d.nspace, lambda k, s: s + jnp.where(owner[k] == me, k, 0), jnp.int32(0))
    row = my_run // d.row_runs
    place = my_run % d.row_runs
    pair = row // 2
    start = jnp.int32(0)
    total = jnp.int32(0)
    for r in range(d.row_runs):
        one = lengths[pair, r]
        start = start + jnp.where(place > r, one, 0)
        total = total + one
    length = lengths[pair, place]
    row_count = d.nspace // d.row_runs
    tab[0] = length
    tab[1] = (place > 0).astype(jnp.int32)
    tab[2] = owner[jnp.maximum(my_run - 1, 0)]
    tab[3] = (place < d.row_runs - 1).astype(jnp.int32)
    tab[4] = owner[jnp.minimum(my_run + 1, d.nspace - 1)]
    for side, step in ((0, -1), (1, 1)):
        target = row + step
        valid = (target >= 0) & (target < row_count)
        there = jnp.clip(target, 0, row_count - 1)
        base = d.t_send + side * (1 + d.row_runs)
        tab[base] = valid.astype(jnp.int32)
        for r in range(d.row_runs):
            tab[base + 1 + r] = owner[there * d.row_runs + r]
        starts = []
        at = jnp.int32(0)
        for r in range(d.row_runs):
            starts.append(at)
            at = at + lengths[there // 2, r]
        for n in range(d.slots + 2):
            s = n - 1
            p = start + s
            ok = valid & (p >= 0) & (p < total) & (s <= length)
            run, first = jnp.int32(0), jnp.int32(0)
            for r in range(1, d.row_runs):
                past = starts[r] <= p
                run = jnp.where(past, r, run)
                first = jnp.where(past, starts[r], first)
            base = d.t_recv + (side * (d.slots + 2) + n) * 3
            tab[base] = ok.astype(jnp.int32)
            tab[base + 1] = owner[there * d.row_runs + run]
            tab[base + 2] = jnp.where(ok, p - first, 0)


def write_shares(d, packed, used, share, send):
    rest = d.nspace * share - used
    if rest:
        packed[used:, :] = jnp.zeros((rest, d.channels), F32)

    def put(n, carry):
        at = pl.multiple_of(n * share, SUB)
        send[n, d.block :, :] = packed[pl.ds(at, share), :].astype(BF)
        return carry

    lax.fori_loop(0, d.nspace, put, 0)


def sum_shares(d, share, recv):
    def add(n, total):
        return total + recv[n, d.block :, :].astype(F32)

    return lax.fori_loop(0, d.nspace, add, jnp.zeros((share, d.channels), F32))


def write_send(d, tab, own, send):
    for side, line in ((0, 0), (1, d.edge - 1)):
        base = d.t_send + side * (1 + d.row_runs)
        blocks = []
        for s in range(d.slots):
            at = line * d.width + s * d.edge
            blocks.append(
                jnp.concatenate([own[q, at : at + d.edge, :] for q in range(d.tiles)], axis=0).astype(BF)
            )

        @pl.when(tab[base] == 1)
        def _(base=base, blocks=blocks):
            for r in range(d.row_runs):
                for s in range(d.slots):
                    send[tab[base + 1 + r], s * d.part : (s + 1) * d.part, :] = blocks[s]

    length = tab[0]
    for flag, to, at in ((1, 2, 0), (3, 4, length * d.edge - 1)):
        end = jnp.concatenate(
            [own[q, pl.ds(at, d.edge, stride=d.width), :] for q in range(d.tiles)], axis=0
        ).astype(BF)

        @pl.when(tab[flag] == 1)
        def _(to=to, end=end):
            send[tab[to], : d.part, :] = end


def fill(d, tab, own, recv, wide, even, odd):
    length = tab[0]
    for q in range(d.tiles):
        zero = jnp.zeros((SUB, d.lanes), F32)
        wide[q, :SUB, :] = zero
        for n in range(d.lines):
            at = SUB + d.line * n + d.width
            wide[q, at : at + SUB, :] = zero
        value = own[q].astype(F32)
        for c in range(d.edge):
            at = SUB + d.line * (c + 1)
            wide[q, at : at + d.width, :] = value[c * d.width : (c + 1) * d.width]
    first = SUB + d.line
    for flag, source, at in ((1, 2, first - 1), (3, 4, first + length * d.edge)):
        keep = tab[flag] == 1
        end = recv[tab[source], : d.part, :].astype(F32)
        end = jnp.where(keep, end, 0.0)
        for q in range(d.tiles):
            wide[q, pl.ds(at, d.edge, stride=d.line), :] = end[q * SUB : (q + 1) * SUB]
    sub = lax.broadcasted_iota(jnp.int32, (SUB, d.lanes), 0)
    for side, line in ((0, 0), (1, d.lines - 1)):
        at = SUB + d.line * line
        for n in range(d.slots + 2):
            s = n - 1
            base = d.t_recv + (side * (d.slots + 2) + n) * 3
            keep = tab[base] == 1
            value = recv[tab[base + 1], pl.ds(pl.multiple_of(tab[base + 2] * d.part, d.part), d.part), :]
            value = jnp.where(keep, value.astype(F32), 0.0)
            for q in range(d.tiles):
                part = value[q * SUB : (q + 1) * SUB]
                if s < 0:
                    wide[q, at - 1 : at, :] = part[SUB - 1 : SUB]
                elif s == d.slots:
                    wide[q, at + s * SUB : at + s * SUB + 1, :] = part[0:1]
                else:
                    wide[q, at + s * SUB : (at + s * SUB) + SUB, :] = jnp.where((sub == 0) | (s < length), part, 0.0)
    for di in (-1, 0, 1):
        for q in range(d.tiles):
            lines = [
                wide[q, SUB + d.line * n + di : SUB + d.line * n + di + d.width, :] for n in range(d.lines)
            ]
            even[di + 1, q] = jnp.concatenate(lines, axis=0).astype(BF)
            odd[di + 1, q] = jnp.concatenate(lines[1:-1], axis=0).astype(BF)


def windows(d, views, direction, q):
    even, odd = views
    parts = []
    for di in (-1, 0, 1):
        for dc in (-1, 0, 1):
            n = 1 + direction * di
            if dc == 0:
                parts.append(odd[n, q])
            else:
                at = d.width * (1 + direction * dc)
                parts.append(even[n, q, at : at + d.rows, :])
    return parts


def beside(ref):
    return jnp.concatenate([ref[n] for n in range(ref.shape[0])], axis=1)


def bands(d, core, flat, inner, outer, outer_t):
    rank, group, lanes = d.rank, d.group, d.lanes
    high = rank // group
    for rh in range(high):
        flat[pl.ds(rh, 27, stride=high), :] = core[:, rh * lanes : (rh + 1) * lanes].astype(F32)
    rows = flat[...].astype(BF)
    at = lax.broadcasted_iota(jnp.int32, (lanes, lanes), 0)
    to = lax.broadcasted_iota(jnp.int32, (lanes, lanes), 1)
    spread = []
    for rl in range(group):
        pick = (at == rl * rank + to % rank).astype(F32).astype(BF)
        spread.append(dot(rows, pick))
    lane = lax.broadcasted_iota(jnp.int32, (rank, lanes), 1) // rank
    zero = jnp.zeros((rank, lanes), BF)
    size = 2 * lanes
    for k in range(d.taps):
        full = []
        for dt in (-1, 0, 1):
            o = 3 * k + dt + 1
            full.append(
                jnp.concatenate([spread[rl][o * high : (o + 1) * high] for rl in range(group)], axis=0)
            )
        cache = {}
        for delta in range(-1, group + 1):
            value = jnp.zeros((rank, lanes), F32)
            for dt in (-1, 0, 1):
                value = jnp.where(lane == delta - dt, full[dt + 1], value)
            cache[delta] = value.astype(BF)
        for down in range(2 * group):
            for across in range(2):
                value = cache.get(down - across * group, zero)
                inner[across, k * size + down * rank : k * size + (down + 1) * rank, :] = value
            far = cache[-1] if down == group - 1 else cache[group] if down == group else zero
            outer_t[k, down * rank : (down + 1) * rank, :] = far
        for down in range(group):
            row = slice(k * lanes + down * rank, k * lanes + (down + 1) * rank)
            outer[0, row, :] = cache[group] if down == 0 else zero
            outer[1, row, :] = cache[-1] if down == group - 1 else zero


class Conv:
    def __init__(self, d, views, inner, outer, direction, out):
        self.d, self.inner, self.direction, self.out = d, inner, direction, out
        self.tiles = [windows(d, views, direction, q) for q in range(d.tiles)]
        self.mul = dot if direction == 1 else dot_nt
        self.half = d.tiles // 2
        lane = lax.broadcasted_iota(jnp.int32, (d.rows, d.lanes), 1) // d.rank
        for p in range(self.half - 1):
            mixed = [
                jnp.where(lane == d.group - 1, x, y)
                for x, y in zip(self.tiles[2 * p + 1], self.tiles[2 * p + 2])
            ]
            total = self.mul(jnp.concatenate(mixed, axis=1), beside(outer))
            for n in range(2):
                out[2 * p + 1 + n] = total[:, n * d.lanes : (n + 1) * d.lanes]

    def left(self, p):
        parts = [
            part for k in range(self.d.taps) for part in (self.tiles[2 * p][k], self.tiles[2 * p + 1][k])
        ]
        return jnp.concatenate(parts, axis=1)

    def put(self, p, total):
        d = self.d
        for n in range(2):
            q = 2 * p + n
            part = total[:, n * d.lanes : (n + 1) * d.lanes]
            if 0 < q < d.tiles - 1:
                part = self.out[q] + part
            self.out[q] = part

    def tile(self, q):
        d = self.d
        if self.direction == 1 and q % 2 == 0:
            self.put(q // 2, dot(self.left(q // 2), beside(self.inner)))
        if self.direction == -1 and q == 0:
            size = 2 * d.lanes
            right = jnp.concatenate(
                [self.inner[n, k * size : (k + 1) * size, :] for k in range(d.taps) for n in range(2)], axis=1
            )
            total = dot_nt(jnp.concatenate([self.left(p) for p in range(self.half)], axis=0), right)
            for p in range(self.half):
                self.put(p, total[p * d.rows : (p + 1) * d.rows])
        return self.out[q]


def core_gradient(d, views, own, out):
    lane = lax.broadcasted_iota(jnp.int32, (1, d.lanes), 1) // d.rank
    tiles = [own[q].astype(F32) for q in range(d.tiles)]
    right = []
    zero = jnp.zeros_like(tiles[0])
    for q in range(d.tiles):
        after = tiles[q + 1] if q + 1 < d.tiles else zero
        before = tiles[q - 1] if q > 0 else zero
        mixed = jnp.where(lane == 0, after, jnp.where(lane == d.group - 1, before, 0.0))
        right.append(jnp.concatenate([tiles[q], mixed], axis=1).astype(BF))
    right = jnp.concatenate(right, axis=0)
    rank, group = d.rank, d.group
    high = rank // group
    wide_lane = lax.broadcasted_iota(jnp.int32, (high, d.lanes), 1) // rank
    left = [jnp.concatenate(windows(d, views, 1, q), axis=1) for q in range(d.tiles)]
    every = dot_tn(jnp.concatenate(left, axis=0), right)
    for k in range(d.taps):
        total = every[k * d.lanes : (k + 1) * d.lanes]
        for dt in (-1, 0, 1):
            pieces = []
            for j in range(group):
                if 0 <= j + dt < group:
                    row, col = j + dt, 0
                elif j + dt == group:
                    row, col = 0, 1
                else:
                    row, col = group - 1, 1
                pieces.append(total[row * rank : (row + 1) * rank, col * d.lanes : (col + 1) * d.lanes])
            result = None
            for turn in range(group):
                mix = None
                for j in range(group):
                    rl = (j + turn) % group
                    part = pieces[j][rl * high : (rl + 1) * high]
                    mix = part if mix is None else jnp.where(wide_lane == j, part, mix)
                if turn:
                    mix = pltpu.roll(mix, turn * rank, 1)
                result = mix if result is None else result + mix
            o = 3 * k + dt + 1
            out[o * high : (o + 1) * high, :] = result


class Copies:
    def __init__(self, sems, pairs):
        self.all = [pltpu.make_async_copy(a, b, sems.at[n]) for n, (a, b) in enumerate(pairs)]
        for one in self.all:
            one.start()

    def wait(self, *which):
        for n in which:
            self.all[n].wait()


def start_kernel(d, me, token):
    token[...] = jnp.zeros((SUB, d.lanes), F32) + me[0].astype(F32)


def first_kernel(
    d, me, lengths_hbm, owner_hbm, x_hbm, reduce_hbm, core_one_hbm, core_two_hbm, token, *refs
):
    del token
    tab_out, xt, own_out, send = refs[:4]
    band_refs = refs[4:10]
    xc, xf, own, lengths, owner, reduce_ref, core_one, core_two, flat, tab, sems = refs[10:]
    copies = Copies(
        sems,
        [
            (lengths_hbm, lengths), (owner_hbm, owner), (reduce_hbm, reduce_ref), (core_one_hbm, core_one),
            (core_two_hbm, core_two),
        ]
        + [(x_hbm.at[:, :, c], xc.at[c]) for c in range(d.edge)],
    )
    copies.wait(0, 1, 2, 3, 4)
    make_table(d, me[0], lengths, owner, tab)
    weight = block_diag(d, permuted_rows(d, reduce_ref[...]))
    save = pltpu.make_async_copy(tab, tab_out, sems.at[d.edge + 5])
    save.start()
    per_line = d.width * d.times
    copies.wait(*range(5, 5 + d.edge))
    for c in range(d.edge):
        xf[c * per_line : (c + 1) * per_line, :] = xc[c].reshape(per_line, d.channels).astype(F32)
    alive = alive_mask(d, tab[0])
    for q in range(d.tiles):
        parts = []
        for j in range(d.group):
            t = q * d.group + j
            parts.append(xf[pl.ds(t, d.rows, stride=d.times), :].astype(BF))
            xt[t] = parts[-1]
        value = dot_nt(jnp.concatenate(parts, axis=1), weight)
        value = jnp.where(alive, value, 0.0).astype(BF)
        own_out[q] = value
        own[q] = value.astype(F32)
        if q == 0:
            bands(d, core_one, flat, *band_refs[0:3])
        if q == d.tiles // 2:
            bands(d, core_two, flat, *band_refs[3:6])
    write_send(d, tab, own, send)
    save.wait()


def layer_one_kernel(
    d, tab_in, own_in, recv, inner, outer, expand_ref, reduce_next, source, mixed, hidden, own_out, send, even, odd,
    wide, conv, own, tab, sems,
):
    Copies(sems, [(tab_in, tab)]).wait(0)
    fill(d, tab, own_in, recv, wide, even, odd)
    mixing = Conv(d, (even, odd), inner, outer, 1, conv)
    expand = block_diag(d, expand_ref[...])
    half = halved(expand)
    weight = block_diag(d, permuted_rows(d, reduce_next[...]))
    alive = alive_mask(d, tab[0])
    for q in range(d.tiles):
        b = mixing.tile(q).astype(BF)
        mixed[q] = b
        y = dot(b, half)
        parts = []
        for j in range(d.group):
            t = q * d.group + j
            u = y[:, j * d.channels : (j + 1) * d.channels]
            parts.append((source[t].astype(F32) + silu(u)).astype(BF))
            hidden[t] = parts[-1]
        value = dot_nt(jnp.concatenate(parts, axis=1), weight)
        value = jnp.where(alive, value, 0.0).astype(BF)
        own_out[q] = value
        own[q] = value.astype(F32)
    write_send(d, tab, own, send)


def read_labels(d, labels, plane):
    for i in range(d.edge):
        part = labels[:, i * d.lanes : (i + 1) * d.lanes].astype(F32)
        plane[pl.ds(i, d.slots, stride=d.edge), :] = part
    value = plane[...]
    lines = [value if c == 0 else pltpu.roll(value, d.lanes - c * d.times, 1) for c in range(d.edge)]
    return jnp.concatenate(lines, axis=0)


def write_prob(d, chance, plane, prob):
    total = chance[: d.width]
    for c in range(1, d.edge):
        total = total + pltpu.roll(chance[c * d.width : (c + 1) * d.width], c * d.times, 1)
    plane[...] = total
    for i in range(d.edge):
        prob[:, i * d.lanes : (i + 1) * d.lanes] = plane[pl.ds(i, d.slots, stride=d.edge), :]


def layer_two_kernel(
    d, tab_in, own_in, recv, inner, outer, expand_ref, head_ref, source, labels, own_out, send, prob, g_out,
    wide, even, odd, conv, own, slope, last, mixed, plane, packed, tab, sems,
):
    Copies(sems, [(tab_in, tab)]).wait(0)
    fill(d, tab, own_in, recv, wide, even, odd)
    mixing = Conv(d, (even, odd), inner, outer, 1, conv)
    expand = block_diag(d, expand_ref[...])
    half = halved(expand)
    head = head_ref[...]
    logit = jnp.zeros((d.rows, d.lanes), F32)
    for q in range(d.tiles):
        b = mixing.tile(q).astype(BF)
        mixed[q] = b
        y = dot(b, half)
        parts = []
        for j in range(d.group):
            t = q * d.group + j
            u = y[:, j * d.channels : (j + 1) * d.channels]
            th = jnp.tanh(u)
            slope[t] = slope_twice(u, th)
            parts.append((source[t].astype(F32) + (u + u * th)).astype(BF))
            last[t] = parts[-1]
        logit = logit + dot_nt(jnp.concatenate(parts, axis=1), head_rows(d, head, q, False))
    chance = jax.nn.sigmoid(logit)
    lane = lax.broadcasted_iota(jnp.int32, (d.rows, d.lanes), 1)
    live = alive_mask(d, tab[0]) & (lane < d.times)
    chance = jnp.where(live, chance, 0.0)
    write_prob(d, chance, plane, prob)
    g = jnp.where(live, chance - read_labels(d, labels, plane), 0.0)
    coarse = g.astype(BF).astype(F32)
    pair = (coarse + pltpu.roll(g - coarse, d.times, 1)).astype(BF)
    g_out[...] = pair
    grad_e = jnp.zeros((d.rank, d.channels), F32)
    grad_h = jnp.zeros((1, d.channels), F32)
    for q in range(d.tiles):
        up = dot(pair, halved(head_rows(d, head, q, True)))
        delta = jnp.concatenate(
            [
                up[:, j * d.channels : (j + 1) * d.channels] * slope[q * d.group + j]
                for j in range(d.group)
            ],
            axis=1,
        ).astype(BF)
        value = dot_nt(delta, expand).astype(BF)
        own_out[q] = value
        own[q] = value.astype(F32)
        grad_e = grad_e + diag_sum(d, dot_tn(mixed[q], delta))
        total = dot_tn(pair, times_of(d, last, q))
        for j in range(d.group):
            t = q * d.group + j
            at = slice(j * d.channels, (j + 1) * d.channels)
            grad_h = grad_h + total[t : t + 1, at] + total[d.times + t : d.times + t + 1, at]
    off = d.two
    core_gradient(d, (even, odd), own_out, packed)
    packed[off[1] : off[2], :] = grad_e
    packed[off[2] : off[3], :] = jnp.concatenate([grad_h, jnp.zeros((SUB - 1, d.channels), F32)], axis=0)
    write_send(d, tab, own, send)
    write_shares(d, packed, off[-1], d.share_two, send)


def back_two_kernel(
    d, tab_in, own_in, recv, inner, outer, reduce_ref, expand_ref, head_ref, source, mixed, g_in, first_even, first_odd,
    own_out, send, shares, wide, even, odd, conv, own, packed, tab, sems,
):
    Copies(sems, [(tab_in, tab)]).wait(0)
    fill(d, tab, own_in, recv, wide, even, odd)
    mixing = Conv(d, (even, odd), inner, outer, -1, conv)
    expand = block_diag(d, expand_ref[...])
    half = halved(expand)
    weight = block_diag(d, permuted_rows(d, reduce_ref[...]))
    head = head_ref[...]
    alive = alive_mask(d, tab[0])
    pair = g_in[...]
    grad_r = jnp.zeros((d.rank, d.channels), F32)
    grad_e = jnp.zeros((d.rank, d.channels), F32)
    for q in range(d.tiles):
        da = jnp.where(alive, mixing.tile(q), 0.0).astype(BF)
        grad_r = grad_r + diag_sum(d, dot_tn(da, times_of(d, source, q)))
        up = dot(
            jnp.concatenate([da, pair], axis=1),
            halved(jnp.concatenate([weight, head_rows(d, head, q, True)], axis=0)),
        )
        b = mixed[q]
        y = dot(b, half)
        parts = []
        for j in range(d.group):
            at = slice(j * d.channels, (j + 1) * d.channels)
            u = y[:, at]
            parts.append((up[:, at] * slope_twice(u, jnp.tanh(u))).astype(BF))
        delta = jnp.concatenate(parts, axis=1)
        value = dot_nt(delta, expand).astype(BF)
        own_out[q] = value
        own[q] = value.astype(F32)
        grad_e = grad_e + diag_sum(d, dot_tn(b, delta))
    off = d.one
    core_gradient(d, (first_even, first_odd), own_out, packed)
    packed[off[1] : off[2], :] = grad_e
    packed[off[2] : off[3], :] = grad_r
    write_send(d, tab, own, send)
    write_shares(d, packed, off[-1], d.share_one, send)
    shares[...] = sum_shares(d, d.share_two, recv)


def back_one_kernel(d, tab_in, own_in, recv, inner, outer, source, shares, send, wide, even, odd, conv, tab, sems):
    Copies(sems, [(tab_in, tab)]).wait(0)
    fill(d, tab, own_in, recv, wide, even, odd)
    mixing = Conv(d, (even, odd), inner, outer, -1, conv)
    alive = alive_mask(d, tab[0])
    grad_r = jnp.zeros((d.rank, d.channels), F32)
    for q in range(d.tiles):
        da = jnp.where(alive, mixing.tile(q), 0.0).astype(BF)
        grad_r = grad_r + diag_sum(d, dot_tn(da, times_of(d, source, q)))

    out = jnp.concatenate([grad_r, shares[...], sum_shares(d, d.share_one, recv)], axis=0).astype(BF)

    def put(n, carry):
        send[n] = out
        return carry

    lax.fori_loop(0, d.nspace, put, 0)


def unpack_kernel(
    d, recv, reduce_one, core_one, expand_one, reduce_two, core_two, expand_two, head, pack_one, pack_two
):
    high = d.rank // d.group
    scale = 1.0 / d.cells
    middle = d.rank + d.share_two

    def take(n, total):
        at = pl.multiple_of(n * d.share_two, SUB)
        pack_two[pl.ds(at, d.share_two), :] = recv[n, d.rank : middle, :].astype(F32) * scale
        at = pl.multiple_of(n * d.share_one, SUB)
        pack_one[pl.ds(at, d.share_one), :] = recv[n, middle:, :].astype(F32) * scale
        return total + recv[n, : d.rank, :].astype(F32)

    first = lax.fori_loop(0, d.nspace, take, jnp.zeros((d.rank, d.channels), F32)) * scale
    for packed, core in ((pack_one, core_one), (pack_two, core_two)):
        for rh in range(high):
            core[:, rh * d.lanes : (rh + 1) * d.lanes] = packed[pl.ds(rh, 27, stride=high), :]
    second = pack_one[d.one[2] : d.one[3], :]
    for value, ref in ((first, reduce_one), (second, reduce_two)):
        for rl in range(d.group):
            ref[pl.ds(rl, high, stride=d.group), :] = value[rl * high : (rl + 1) * high]
    expand_one[...] = pack_one[d.one[1] : d.one[2], :]
    expand_two[...] = pack_two[d.two[1] : d.two[2], :]
    head[...] = pack_two[d.two[2] : d.two[2] + 1, :]


VM = pl.BlockSpec(memory_space=pltpu.VMEM)
SM = pl.BlockSpec(memory_space=pltpu.SMEM)
HB = pl.BlockSpec(memory_space=pltpu.HBM)


def call(kernel, d, name, ins, outs, scratch, operands, cost=None):
    shapes = tuple(jax.ShapeDtypeStruct(s, t) for s, t, _ in outs)
    specs = tuple(m for _, _, m in outs)
    return pl.pallas_call(
        functools.partial(kernel, d),
        out_shape=shapes,
        in_specs=list(ins),
        out_specs=specs,
        scratch_shapes=scratch,
        name=name,
        cost_estimate=cost,
        compiler_params=pltpu.CompilerParams(vmem_limit_bytes=LIMIT),
    )(*operands)


def on_device(
    volume, labels, run_lengths, run_owner, reduce_one, core_one, expand_one, reduce_two, core_two, expand_two,
    head_vector,
):
    nspace = lax.axis_size("space")
    slots, edge, _, times, channels = volume.shape
    rank = reduce_one.shape[0]
    d = Dims(nspace, slots, edge, times, channels, rank, run_lengths.shape[0], run_lengths.shape[1])
    me = lax.axis_index("space").astype(jnp.int32).reshape(1)
    head = head_vector.reshape(1, channels)
    own_shape = (d.tiles, d.rows, d.lanes)
    wide_shape = (d.times, d.rows, d.channels)
    send_shape = (nspace, d.block, channels)
    even_shape = (3, d.tiles, d.lines * d.width, d.lanes)
    odd_shape = (3, d.tiles, d.rows, d.lanes)
    size = 2 * d.lanes
    core_shape = (27 * rank // d.group, d.lanes)
    own_f = pltpu.VMEM(own_shape, F32)
    rim = pltpu.VMEM((d.tiles, d.span + 2 * SUB, d.lanes), F32)
    views = [pltpu.VMEM(even_shape, BF), pltpu.VMEM(odd_shape, BF)]
    tab_s = pltpu.SMEM((d.t_size,), jnp.int32)
    small = ((rank, channels), F32, VM)
    own_o, wide_o, send_o = (own_shape, BF, VM), (wide_shape, BF, VM), (send_shape, BF, VM)
    band_shapes = [
        (2, d.taps * size, d.lanes), (2, d.taps * d.lanes, d.lanes), (d.taps, size, d.lanes)
    ] * 2
    pack_one = pltpu.VMEM((nspace * d.share_one, channels), F32)
    pack_two = pltpu.VMEM((nspace * d.share_two, channels), F32)

    def sems(n):
        return pltpu.SemaphoreType.DMA((n,))

    def exchange(send):
        return lax.all_to_all(send, "space", split_axis=0, concat_axis=0, tiled=True)

    (token,) = call(
        start_kernel, d, "start", [SM], [((SUB, d.lanes), F32, VM)], [], [me],
        cost=pl.CostEstimate(flops=10**10, bytes_accessed=0, transcendentals=0),
    )
    tab, xt, a1, send, inner1, outer1, outer1t, inner2, outer2, outer2t = call(
        first_kernel, d, "first", [SM] + [HB] * 6 + [VM],
        [((d.t_size,), jnp.int32, VM), wide_o, own_o, send_o] + [(b, BF, VM) for b in band_shapes],
        [
            pltpu.VMEM((edge, slots, edge, times, channels), BF),
            pltpu.VMEM((d.rows * times, channels), F32),
            own_f, pltpu.SMEM(run_lengths.shape, jnp.int32), pltpu.SMEM(run_owner.shape, jnp.int32),
            pltpu.VMEM((rank, channels), BF), pltpu.VMEM(core_one.shape, BF), pltpu.VMEM(core_one.shape, BF),
            pltpu.VMEM(core_shape, F32), tab_s, sems(edge + 6),
        ],
        [me, run_lengths, run_owner, volume, reduce_one, core_one, core_two, token],
    )
    recv = exchange(send)
    b1, h1, a2, send, even1, odd1 = call(
        layer_one_kernel, d, "layer_one", [VM] * 8,
        [own_o, wide_o, own_o, send_o, (even_shape, BF, VM), (odd_shape, BF, VM)],
        [rim, own_f, own_f, tab_s, sems(1)],
        [tab, a1, recv, inner1, outer1, expand_one, reduce_two, xt],
    )
    recv = exchange(send)
    db2, send, prob, g = call(
        layer_two_kernel, d, "layer_two", [VM] * 9,
        [
            own_o, ((nspace, d.block + d.share_two, channels), BF, VM), (labels.shape, F32, VM),
            ((d.rows, d.lanes), BF, VM),
        ],
        [rim]
        + views
        + [
            own_f, own_f, pltpu.VMEM(wide_shape, F32), pltpu.VMEM(wide_shape, BF), pltpu.VMEM(own_shape, BF),
            pltpu.VMEM((d.width, d.lanes), F32), pack_two, tab_s, sems(1),
        ],
        [tab, a2, recv, inner2, outer2, expand_two, head, h1, labels],
    )
    recv = exchange(send)
    db1, send, shares = call(
        back_two_kernel, d, "back_two", [VM] * 13,
        [own_o, ((nspace, d.block + d.share_one, channels), BF, VM), ((d.share_two, channels), F32, VM)],
        [rim] + views + [own_f, own_f, pack_one, tab_s, sems(1)],
        [tab, db2, recv, inner2, outer2t, reduce_two, expand_one, head, h1, b1, g, even1, odd1],
    )
    recv = exchange(send)
    (send,) = call(
        back_one_kernel, d, "back_one", [VM] * 7,
        [((nspace, rank + d.share_two + d.share_one, channels), BF, VM)],
        [rim] + views + [own_f, tab_s, sems(1)],
        [tab, db1, recv, inner1, outer1t, xt, shares],
    )
    recv = exchange(send)
    core_out = ((27, rank * rank), F32, VM)
    r1, c1, e1, r2, c2, e2, hv = call(
        unpack_kernel, d, "unpack", [VM],
        [small, core_out, small, small, core_out, small, ((1, channels), F32, VM)],
        [pack_one, pack_two], [recv],
    )
    return prob, r1, c1, e1, r2, c2, e2, hv.reshape(channels)


def solution(mesh):
    in_specs = (
        P(("groups", "space"), None, None, None, None),
        P(("groups", "space"), None),
        P("groups", None),
        P("groups"),
    ) + (P(),) * 7
    out_specs = (P(("groups", "space"), None),) + (P("groups", None),) * 6 + (P("groups"),)
    return jax.shard_map(on_device, mesh=mesh, in_specs=in_specs, out_specs=out_specs, check_vma=False)
```
